32 devices in a mesh: group: 8 (over y, x, core), member: 4 (over z).
Axes of the slice: x: 2, y: 2, z: 4, core: 2. Of those that a mesh axis runs over, the one named last changes fastest.
Arguments:
- tokens: bfloat16 [4096, 2048], P(('group', 'member')), may hold values from -6 to 6
- grad_out: bfloat16 [4096, 2048], P(('group', 'member')), may hold values from -6 to 6
- expert_ids: int32 [4096, 8], P(('group', 'member')), may hold values from 0 to 31, as said below
- pair_slot: int32 [4096, 8], P(('group', 'member')), may hold values from 0 to 47, as said below
- gate_weights: bfloat16 [4096, 8], P(('group', 'member')), may hold values from 0.049804688 to 1
- weight_gate: bfloat16 [32, 2048, 768], P(('group', 'member')), may hold values from -0.125 to 0.125
- weight_up: bfloat16 [32, 2048, 768], P(('group', 'member')), may hold values from -0.125 to 0.125
- weight_down: bfloat16 [32, 768, 2048], P(('group', 'member')), may hold values from -0.21875 to 0.21875
- saved_gate: bfloat16 [32, 1536, 768], P(('group', 'member')), may hold values from -6 to 6
- saved_up: bfloat16 [32, 1536, 768], P(('group', 'member')), may hold values from -6 to 6
Outputs:
- grad_tokens: bfloat16 [4096, 2048], P(('group', 'member'))
- grad_gates: bfloat16 [4096, 8], P(('group', 'member'))
- grad_weight_gate: bfloat16 [32, 2048, 768], P(('group', 'member'))
- grad_weight_up: bfloat16 [32, 2048, 768], P(('group', 'member'))
- grad_weight_down: bfloat16 [32, 768, 2048], P(('group', 'member'))
The draws below stay inside these ranges and needn't reach their ends.
Inputs may be any that keep to these rules, and one draw needn't show every extreme that they name: `expert_ids`: each token names 8 distinct experts, two in each of exactly 4 groups, the group of expert e being e // 4. The tokens of one device send at most 96 tokens to one group, and in every draw some group gets exactly 96 from every device. `pair_slot`: among one device's assignments to one expert the slots are distinct and run from 0 to their count less one, in no fixed order of tokens. In every draw some expert gets exactly 48 assignments from every device.
All inputs are finite; a program needn't handle non-finite values.
Results may differ from the reference program's by a relative error of at most 0.012.
Values may be sent and summed in bfloat16 or wider, within the bound.
A program may use at most 192 MiB of HBM per device.

```python
import math
import jax
import jax.numpy as jnp
from jax import lax

D = 2048
FF = 768
TOP = 8
GROUP_VISITS = 4
TOK_DEV = 128
GROUPS = 8
MEMBERS = 4
EXPERTS = 32
TOKENS = 4096
PAIR = 48
CAP = 1536
GROUP_SLOTS = 96


def routing_tables(key):
    base_key = jax.random.fold_in(key, 11)
    key_pop, key_hot, key_member, key_devices = jax.random.split(base_key, 4)
    expert_preference = jax.random.randint(key_pop, (GROUPS,), 0, 2048, dtype=jnp.int32)
    favored_group = jax.random.randint(key_hot, (), 0, GROUPS, dtype=jnp.int32)
    hot_member = jax.random.randint(key_member, (), 0, MEMBERS, dtype=jnp.int32)
    group_indices = jnp.arange(GROUPS, dtype=jnp.int32)
    member_range = jnp.arange(MEMBERS, dtype=jnp.int32)
    group_extra_score = expert_preference + jnp.where(group_indices == favored_group, 1 << 20, 0)

    def token_step(carry, token_key):
        group_total, expert_count = carry
        key_groups, key_experts = jax.random.split(token_key)
        group_jitter = jax.random.randint(key_groups, (GROUPS,), 0, 1024, dtype=jnp.int32)
        expert_noise = jax.random.randint(key_experts, (EXPERTS,), 0, 1024, dtype=jnp.int32)
        group_affinity = jnp.where(group_total < GROUP_SLOTS, group_extra_score + group_jitter - group_total * 1024, -(1 << 23)) * 64 + group_indices
        chosen_groups = lax.top_k(group_affinity, GROUP_VISITS)[1]
        chosen_experts = []
        chosen_slots = []
        for visit_number in range(GROUP_VISITS):
            group_pick = chosen_groups[visit_number]
            first_expert = group_pick * MEMBERS
            counts = lax.dynamic_slice(expert_count, (first_expert,), (MEMBERS,))
            noise_here = lax.dynamic_slice(expert_noise, (first_expert,), (MEMBERS,))
            hot_boost = jnp.where((group_pick == favored_group) & (member_range == hot_member), 1 << 22, 0)
            expert_score = jnp.where(counts < PAIR, noise_here - counts * 2048 + hot_boost, -(1 << 24)) * 64 + member_range
            picked = lax.top_k(expert_score, 2)[1]
            chosen_experts.append(first_expert + picked)
            chosen_slots.append(counts[picked])
            expert_count = expert_count.at[first_expert + picked].add(1)
            group_total = group_total.at[group_pick].add(1)
        return ((group_total, expert_count), (jnp.concatenate(chosen_experts), jnp.concatenate(chosen_slots)))

    def one_device(device_key):
        key_tokens, key_order = jax.random.split(device_key)
        start_carry = (jnp.zeros((GROUPS,), jnp.int32), jnp.zeros((EXPERTS,), jnp.int32))
        tables = lax.scan(token_step, start_carry, jax.random.split(key_tokens, TOK_DEV))[1]
        order = jax.random.permutation(key_order, TOK_DEV)
        return (tables[0][order], tables[1][order])
    experts_all, slots_all = jax.vmap(one_device)(jax.random.split(key_devices, EXPERTS))
    return (experts_all.reshape(TOKENS, TOP).astype(jnp.int32), slots_all.reshape(TOKENS, TOP).astype(jnp.int32))


def draw_expert_ids(key, part):
    return routing_tables(key)[0]


def draw_pair_slot(key, part):
    return routing_tables(key)[1]


def level_of(stream_key, shape, shards, low, top_value):
    def one(position, parts):
        steps = jax.random.uniform(jax.random.fold_in(jax.random.fold_in(stream_key, 6), position), (parts,), jnp.float32, low / len(shards), top_value / len(shards))
        return jnp.repeat(jnp.exp(steps), shape[position] // parts).reshape((-1,) + (1,) * (len(shape) - position - 1))

    gain = one(*shards[0])
    for cut in shards[1:]:
        gain = gain * one(*cut)
    return gain


def gaussian(stream_key, shape, deviation, reach, cuts=(), held_as=jnp.bfloat16):
    factor_of = level_of(stream_key, shape, cuts, -0.22, 0.18) if cuts else 1.0
    entries = jax.random.normal(stream_key, shape, jnp.float32) * deviation * factor_of
    return jnp.minimum(jnp.maximum(entries, -reach), reach).astype(held_as)


def setup_inputs(seed: int = 0) -> dict:
    key_of = jax.random.split(jax.random.key(seed), 11)
    tokens = gaussian(key_of[0], (TOKENS, D), 1.0, 6.0, ((0, 32),))
    grad_out = gaussian(key_of[1], (TOKENS, D), 1.0, 6.0, ((0, 32),))
    expert_ids = draw_expert_ids(jax.random.fold_in(key_of[10], 71), 0)
    pair_slot = draw_pair_slot(jax.random.fold_in(key_of[10], 71), 0)
    gate_weights = jnp.clip(jnp.exp(math.log(1.0) - 2.9996462 * jax.random.uniform(key_of[4], (TOKENS, TOP), jnp.float32) ** level_of(key_of[4], (TOKENS, TOP), ((0, 32),), -0.2, 0.2)), 0.049804688, 1.0).astype(jnp.bfloat16)
    weight_gate = gaussian(key_of[5], (EXPERTS, D, FF), D ** -0.5, 0.125, ((0, 32),))
    weight_up = gaussian(key_of[6], (EXPERTS, D, FF), D ** -0.5, 0.125, ((0, 32),))
    weight_down = gaussian(key_of[7], (EXPERTS, FF, D), FF ** -0.5, 0.21875, ((0, 32),))
    saved_gate = gaussian(key_of[8], (EXPERTS, CAP, FF), 1.0, 6.0, ((0, 32),))
    saved_up = gaussian(key_of[9], (EXPERTS, CAP, FF), 1.0, 6.0, ((0, 32),))
    return dict(tokens=tokens, grad_out=grad_out, expert_ids=expert_ids, pair_slot=pair_slot, gate_weights=gate_weights, weight_gate=weight_gate, weight_up=weight_up, weight_down=weight_down, saved_gate=saved_gate, saved_up=saved_up)


def expert_block(token_rows, grad_rows, route_gate, saved_pregate, saved_preup, weight_gate, weight_up, weight_down):
    pre_gate = saved_pregate.astype(jnp.float32)
    pre_up = saved_preup.astype(jnp.float32)
    gate_sigmoid = jax.nn.sigmoid(pre_gate)
    gate_swish = pre_gate * gate_sigmoid
    hidden = gate_swish * pre_up
    hidden_low = hidden.astype(jnp.bfloat16)
    route_scale = route_gate.astype(jnp.float32)[:, None]
    scaled_grads = (route_scale * grad_rows.astype(jnp.float32)).astype(jnp.bfloat16)
    down_grad = jnp.dot(hidden_low.T, scaled_grads, preferred_element_type=jnp.float32)
    back_hidden = jnp.dot(grad_rows, weight_down.T, preferred_element_type=jnp.float32)
    slot_gate = jnp.sum(hidden * back_hidden, axis=1).astype(jnp.bfloat16)
    hidden_grad = route_scale * back_hidden
    pregate_grad = (hidden_grad * pre_up * gate_sigmoid * (1.0 + pre_gate * (1.0 - gate_sigmoid))).astype(jnp.bfloat16)
    preup_grad = (hidden_grad * gate_swish).astype(jnp.bfloat16)
    gate_grad = jnp.dot(token_rows.T, pregate_grad, preferred_element_type=jnp.float32)
    up_grad = jnp.dot(token_rows.T, preup_grad, preferred_element_type=jnp.float32)
    slot_grad = (jnp.dot(pregate_grad, weight_gate.T, preferred_element_type=jnp.float32)
                 + jnp.dot(preup_grad, weight_up.T, preferred_element_type=jnp.float32)).astype(jnp.bfloat16)
    return slot_grad, slot_gate, gate_grad, up_grad, down_grad


def reference(tokens, grad_out, expert_ids, pair_slot, gate_weights, weight_gate, weight_up, weight_down, saved_gate, saved_up):
    route_total = TOKENS * TOP
    route_index = jnp.arange(route_total, dtype=jnp.int32)
    source = (route_index // TOP) // TOK_DEV
    flat_slot = (expert_ids.reshape(-1) * CAP + source * PAIR + pair_slot.reshape(-1)).astype(jnp.int32)
    slot_route = jnp.full((EXPERTS * CAP,), route_total, jnp.int32).at[flat_slot].set(route_index)
    gates_flat = gate_weights.reshape(-1)

    def expert_step(carry, expert):
        token_acc, term_acc = carry
        routes_here = lax.dynamic_slice(slot_route, (expert * CAP,), (CAP,))
        token_here = (routes_here // TOP).astype(jnp.int32)
        rows_here = jnp.take(tokens, token_here, axis=0, mode="fill", fill_value=0)
        grads_here = jnp.take(grad_out, token_here, axis=0, mode="fill", fill_value=0)
        gates_here = jnp.take(gates_flat, routes_here, axis=0, mode="fill", fill_value=0)
        slot_grad, slot_gate, gate_grad, up_grad, down_grad = expert_block(
            rows_here, grads_here, gates_here, saved_gate[expert], saved_up[expert],
            weight_gate[expert], weight_up[expert], weight_down[expert])
        token_acc = token_acc.at[token_here].add(slot_grad.astype(jnp.float32), mode="drop")
        term_acc = term_acc.at[routes_here].set(slot_gate.astype(jnp.float32), mode="drop")
        return (token_acc, term_acc), (gate_grad.astype(jnp.bfloat16), up_grad.astype(jnp.bfloat16), down_grad.astype(jnp.bfloat16))

    start_carry = (jnp.zeros((TOKENS, D), jnp.float32), jnp.zeros((route_total,), jnp.float32))
    final_carry, weight_grads = lax.scan(expert_step, start_carry, jnp.arange(EXPERTS, dtype=jnp.int32))
    token_acc, term_acc = final_carry
    return (token_acc.astype(jnp.bfloat16), term_acc.reshape(TOKENS, TOP).astype(jnp.bfloat16),
            weight_grads[0], weight_grads[1], weight_grads[2])
```

```python
import jax
import jax.numpy as jnp
from jax import lax
from jax.experimental import pallas as pl
from jax.experimental.pallas import tpu as pltpu
from jax.sharding import PartitionSpec as P

AXES = ("group", "member")
OVER_ROWS = (((0,), (0,)), ((), ()))


def expert_block(
    token_rows,
    grad_rows,
    route_gate,
    saved_pregate,
    saved_preup,
    weight_gate,
    weight_up,
    weight_down,
):
    pre_gate = saved_pregate.astype(jnp.float32)
    pre_up = saved_preup.astype(jnp.float32)
    gate_sigmoid = jax.nn.sigmoid(pre_gate)
    gate_swish = pre_gate * gate_sigmoid
    hidden = gate_swish * pre_up
    hidden_low = hidden.astype(jnp.bfloat16)
    route_scale = route_gate.astype(jnp.float32)[:, None]
    scaled_grads = (route_scale * grad_rows.astype(jnp.float32)).astype(jnp.bfloat16)
    over_rows = (((0,), (0,)), ((), ()))
    over_features = (((1,), (1,)), ((), ()))
    down_grad = lax.dot_general(
        hidden_low, scaled_grads, over_rows, preferred_element_type=jnp.float32
    )
    back_hidden = lax.dot_general(
        grad_rows, weight_down, over_features, preferred_element_type=jnp.float32
    )
    slot_gate = jnp.sum(hidden * back_hidden, axis=1).astype(jnp.bfloat16)
    hidden_grad = route_scale * back_hidden
    pregate_grad = (
        hidden_grad * pre_up * gate_sigmoid * (1.0 + pre_gate * (1.0 - gate_sigmoid))
    ).astype(jnp.bfloat16)
    preup_grad = (hidden_grad * gate_swish).astype(jnp.bfloat16)
    gate_grad = lax.dot_general(
        token_rows, pregate_grad, over_rows, preferred_element_type=jnp.float32
    )
    up_grad = lax.dot_general(token_rows, preup_grad, over_rows, preferred_element_type=jnp.float32)
    slot_grad = (
        lax.dot_general(
            pregate_grad, weight_gate, over_features, preferred_element_type=jnp.float32
        )
        + lax.dot_general(preup_grad, weight_up, over_features, preferred_element_type=jnp.float32)
    ).astype(jnp.bfloat16)
    return (slot_grad, slot_gate, gate_grad, up_grad, down_grad)


def pair_body(
    tokens,
    grad_out,
    expert_ids,
    pair_slot,
    gate_weights,
    weight_gate,
    weight_up,
    weight_down,
    saved_gate,
    saved_up,
):
    groups = lax.axis_size("group")
    members = lax.axis_size("member")
    experts = groups * members
    tok_rows, model_width = tokens.shape
    route_count = expert_ids.shape[1]
    capacity = saved_gate.shape[1]
    pair_rows = capacity // experts
    token_range = jnp.arange(tok_rows, dtype=jnp.int32)
    dest = (expert_ids * pair_rows + pair_slot).reshape(-1)
    slot_token = (
        jnp.full((experts * pair_rows,), tok_rows, jnp.int32)
        .at[dest]
        .set(jnp.repeat(token_range, route_count))
    )
    send_rows = jnp.take(tokens, slot_token, axis=0, mode="fill", fill_value=0)
    send_grads = jnp.take(grad_out, slot_token, axis=0, mode="fill", fill_value=0)
    send_gates = (
        jnp.zeros((experts * pair_rows,), jnp.bfloat16).at[dest].set(gate_weights.reshape(-1))
    )
    expert_rows, expert_grads, expert_gates = (
        lax.all_to_all(send_rows, ("group", "member"), split_axis=0, concat_axis=0, tiled=True),
        lax.all_to_all(send_grads, ("group", "member"), split_axis=0, concat_axis=0, tiled=True),
        lax.all_to_all(send_gates, ("group", "member"), split_axis=0, concat_axis=0, tiled=True),
    )
    slot_grad, slot_gate, gate_total, up_total, down_total = expert_block(
        expert_rows,
        expert_grads,
        expert_gates,
        saved_gate[0],
        saved_up[0],
        weight_gate[0],
        weight_up[0],
        weight_down[0],
    )
    back_rows, back_terms = (
        lax.all_to_all(slot_grad, ("group", "member"), split_axis=0, concat_axis=0, tiled=True),
        lax.all_to_all(slot_gate, ("group", "member"), split_axis=0, concat_axis=0, tiled=True),
    )
    per_route = jnp.take(back_rows, dest, axis=0).reshape(tok_rows, route_count, model_width)
    grad_tokens = jnp.sum(per_route.astype(jnp.float32), axis=1).astype(jnp.bfloat16)
    grad_gates = jnp.take(back_terms, dest, axis=0).reshape(tok_rows, route_count)
    return (
        grad_tokens,
        grad_gates,
        gate_total[None].astype(jnp.bfloat16),
        up_total[None].astype(jnp.bfloat16),
        down_total[None].astype(jnp.bfloat16),
    )


MESH_ID = pl.DeviceIdType.MESH
EXT = 128
OVER_LAST = (((1,), (1,)), ((), ()))


def fused_kernel(
    ids_ref, slots_ref, gates_ref, tok_hbm, grd_hbm, wg_hbm, wu_hbm, wd_hbm, sa_hbm, sb_hbm,
    out_tok, out_gate, out_down, token_rows, pre_hbm, up_hbm,
    gd, td, gs, ts, gr, rs, rb, pd, pa, zs, zr, wg, wu, wd, pg, pu, bh, ht, pick_to, pick_from,
    sel, load_sem, row_sem, store_sem,
    z_send, z_recv, a_send, a_recv, c_send, c_recv, r_send, r_recv,
):
    f32, bf16 = jnp.float32, jnp.bfloat16
    tok, width = tok_hbm.shape
    wide = width + EXT
    cap, hid_width = sa_hbm.shape
    part = cap // 4
    four = part // 4
    pair = four // 2
    g, z = lax.axis_index("group"), lax.axis_index("member")
    c, x, y = g % 2, (g // 2) % 2, g // 4
    a, b = x * (1 - c) + y * c, y * (1 - c) + x * c
    me = g * 4 + z

    def place(da, db, dc):
        pa_, pb_ = (1 - a if da else a), (1 - b if db else b)
        pc_ = 1 - c if dc else c
        px, py = pa_ * (1 - c) + pb_ * c, pb_ * (1 - c) + pa_ * c
        return (py * 2 + px) * 2 + pc_

    def plane(k):
        return (z, z + 1 - 2 * (z % 2), (z + 2) % 4, 3 - z)[k]

    lane_to = ((0, 0, 0), (0, 0, 1), (0, 1, 0), (0, 1, 1))
    lane_from = ((0, 0, 0), (0, 0, 1), (0, 1, 0), (1, 0, 1))

    def source(j, i):
        return ((i, 0, 0), (0, i, 1), (i, 1, 0), (1, i, 1))[j]

    def remote(src, dst, ssem, rsem, group, member):
        return pltpu.make_async_remote_copy(
            src_ref=src, dst_ref=dst, send_sem=ssem, recv_sem=rsem,
            device_id=(group, member), device_id_type=MESH_ID,
        )

    dense = (gd, td)

    def z_copy(u, k):
        n = u * 3 + k - 1
        return remote(dense[u].at[0, 0], dense[u].at[k, 0], z_send.at[n], z_recv.at[n], g, plane(k))

    def a_copy(u, k):
        n = u * 4 + k
        return remote(
            dense[u].at[k, 0], dense[u].at[k, 1], a_send.at[n], a_recv.at[n], place(1, 0, 0), z
        )

    def c_copy(u, k, j):
        n = (u * 4 + k) * 3 + j - 1
        src, dst = (gs, gr) if u == 0 else (ts, token_rows)
        return remote(
            src.at[k % 2, pl.ds((j - 1) * four, four)], dst.at[pl.ds(k * part + j * four, four)],
            c_send.at[n], c_recv.at[n], place(*lane_to[j]), z,
        )

    def r_copy(k, j):
        n = k * 3 + j - 1
        return remote(
            rs.at[k % 2, pl.ds((j - 1) * four, four)], rb.at[pl.ds(k * part + j * four, four)],
            r_send.at[n], r_recv.at[n], place(*lane_from[j]), z,
        )

    def pa_copy(k):
        return remote(pd.at[k], pa.at[k], a_send.at[8 + k], a_recv.at[8 + k], place(1, 0, 0), z)

    def pz_copy(k):
        return remote(
            zs.at[k - 1], zr.at[k - 1], z_send.at[5 + k], z_recv.at[5 + k], g, plane(k)
        )

    def own_rows(k):
        return pltpu.make_async_copy(
            ts.at[k % 2, pl.ds(3 * four, four)], token_rows.at[pl.ds(k * part, four)],
            store_sem.at[k],
        )

    load_grd = pltpu.make_async_copy(grd_hbm, gd.at[0, 0, :, pl.ds(0, width)], load_sem.at[0])
    load_tok = pltpu.make_async_copy(tok_hbm, td.at[0, 0], load_sem.at[1])
    load_wd = pltpu.make_async_copy(wd_hbm, wd, load_sem.at[2])
    load_wg = pltpu.make_async_copy(wg_hbm, wg, load_sem.at[3])
    load_wu = pltpu.make_async_copy(wu_hbm, wu, load_sem.at[4])
    load_grd.start()
    load_tok.start()

    barrier = pltpu.get_barrier_semaphore()
    peers = [(place(*p), z) for p in ((1, 0, 0), (1, 0, 1), (0, 1, 0), (0, 1, 1), (0, 0, 1))]
    peers += [(g, plane(k)) for k in (1, 2, 3)]
    for peer in peers:
        pl.semaphore_signal(barrier, inc=1, device_id=peer, device_id_type=MESH_ID)

    lane = lax.broadcasted_iota(jnp.int32, (tok, EXT), 1)
    ext = jnp.zeros((tok, EXT), f32)
    for r in range(ids_ref.shape[1]):
        expert = ids_ref[:, r : r + 1]
        ext += jnp.where(lane == expert, gates_ref[:, r : r + 1].astype(f32), 0.0)
        ext += jnp.where(lane == expert + 32, (slots_ref[:, r : r + 1] + 1).astype(f32), 0.0)
    gd[0, 0, :, width:wide] = ext.astype(bf16)
    lane_pair = lax.broadcasted_iota(jnp.int32, (pair, EXT), 1)
    for j in range(4):
        expert = place(*lane_to[j]) * 4 + z
        sel[j * pair : (j + 1) * pair, :] = jnp.where(lane_pair == expert + 32, 1.0, 0.0).astype(bf16)

    pl.semaphore_wait(barrier, len(peers))
    load_grd.wait()
    for k in (1, 2, 3):
        z_copy(0, k).start()
    a_copy(0, 0).start()
    load_tok.wait()
    a_copy(1, 0).start()
    load_wd.start()
    load_wg.start()
    load_wu.start()
    for k in range(4):
        for j in range(4):
            for i in range(2):
                row = (place(*source(j, i)) * 4 + plane(k)) * pair
                row = pl.ds(pl.multiple_of(row, 16), pair)
                at = pl.ds(k * part + j * four + i * pair, pair)
                pltpu.make_async_copy(sa_hbm.at[row], pg.at[at], row_sem.at[k]).start()
                pltpu.make_async_copy(sb_hbm.at[row], pu.at[at], row_sem.at[4 + k]).start()

    def want(shape, dim):
        at = lax.broadcasted_iota(jnp.int32, shape, dim)
        for _ in range(3):
            at = jnp.where(at >= pair, at - pair, at)
        return (at + 1).astype(f32)

    def gather(u, k):
        if u == 1 and k >= 2:
            own_rows(k - 2).wait()
        if k >= 2:
            for j in (1, 2, 3):
                c_copy(u, k - 2, j).wait_send()
        for i in range(2):
            if u == 0:
                tags = gd[k, i, :, width:wide]
                slot_at = lax.dot_general(sel[...], tags, OVER_LAST, preferred_element_type=f32)
                pick_to[k * 2 + i] = (slot_at == want((4 * pair, tok), 0)).astype(bf16)
                slot_at = lax.dot_general(tags, sel[...], OVER_LAST, preferred_element_type=f32)
                pick_from[k * 2 + i] = (slot_at == want((tok, 4 * pair), 1)).astype(bf16)
            got = jnp.dot(
                pick_to[k * 2 + i], dense[u][k, i], preferred_element_type=f32
            ).astype(bf16)
            if u == 0:
                gr[pl.ds(k * part + i * pair, pair), :] = got[:pair]
            else:
                ts[k % 2, pl.ds(3 * four + i * pair, pair), :] = got[:pair]
            send = gs if u == 0 else ts
            for j in (1, 2, 3):
                send[k % 2, pl.ds((j - 1) * four + i * pair, pair), :] = got[
                    j * pair : (j + 1) * pair
                ]
        for j in (1, 2, 3):
            c_copy(u, k, j).start()
        if u == 1:
            own_rows(k).start()

    def expert(k):
        rows = pl.ds(k * part, part)
        for j in (1, 2, 3):
            c_copy(0, k, j).wait_recv()
        if k == 0:
            load_wd.wait()
            load_wg.wait()
            load_wu.wait()
        pltpu.make_async_copy(sa_hbm.at[pl.ds(0, part)], pg.at[rows], row_sem.at[k]).wait()
        pltpu.make_async_copy(sb_hbm.at[pl.ds(0, part)], pu.at[rows], row_sem.at[4 + k]).wait()

        @pl.loop(0, hid_width // 256)
        def _(n):
            cols = pl.ds(pl.multiple_of(n * 256, 256), 256)
            bh[:, cols] = lax.dot_general(
                gr[rows, :width], wd[cols, :], OVER_LAST, preferred_element_type=f32
            )

        if k >= 2:
            for j in (1, 2, 3):
                r_copy(k - 2, j).wait_send()

        def hidden_rows(j, put):
            at = k * part + j * four
            here = pl.ds(at if isinstance(j, int) else pl.multiple_of(at, 16), four)
            there = pl.ds(j * four if isinstance(j, int) else pl.multiple_of(j * four, 16), four)
            tag = lax.broadcasted_iota(jnp.int32, (four, EXT), 1) == me
            route = jnp.sum(
                jnp.where(tag, gr[here, width:wide].astype(f32), 0.0), axis=1, keepdims=True
            )
            pre, up, back = pg[here, :].astype(f32), pu[here, :].astype(f32), bh[there, :]
            sig = jax.nn.sigmoid(pre)
            swish = pre * sig
            hidden = swish * up
            term = jnp.sum(hidden * back, axis=1, keepdims=True)
            back = route * back
            pg[here, :] = (back * up * sig * (1.0 + pre * (1.0 - sig))).astype(bf16)
            pu[here, :] = (back * swish).astype(bf16)
            bh[there, :] = hidden
            put(jnp.where(tag, term, 0.0).astype(bf16))
            gr[here, :width] = (route * gr[here, :width].astype(f32)).astype(bf16)

        def put_own(value):
            rb[pl.ds(k * part, four), width:wide] = value

        hidden_rows(0, put_own)

        @pl.loop(1, 4)
        def _(j):
            def put_far(value):
                rs[k % 2, pl.ds(pl.multiple_of((j - 1) * four, 16), four), width:wide] = value

            hidden_rows(j, put_far)

        @pl.loop(0, width // 256)
        def _(n):
            cols = pl.ds(pl.multiple_of(n * 256, 256), 256)
            back = lax.dot_general(
                pg[rows, :], wg[cols, :], OVER_LAST, preferred_element_type=f32
            ) + lax.dot_general(pu[rows, :], wu[cols, :], OVER_LAST, preferred_element_type=f32)
            back = back.astype(bf16)
            rb[pl.ds(k * part, four), cols] = back[:four]
            rs[k % 2, :, cols] = back[four:]

        for j in (1, 2, 3):
            r_copy(k, j).start()
        pltpu.make_async_copy(pg.at[rows], pre_hbm.at[rows], store_sem.at[4 + k]).start()
        pltpu.make_async_copy(pu.at[rows], up_hbm.at[rows], store_sem.at[8 + k]).start()
        ht[:, rows] = bh[...].astype(bf16).T

    def spread(k, i):
        got = jnp.concatenate(
            [rb[pl.ds(k * part + j * four + i * pair, pair), :] for j in range(4)], axis=0
        )
        return jnp.dot(pick_from[k * 2 + i], got, preferred_element_type=f32)

    def back_near(k):
        for j in (1, 2, 3):
            r_copy(k, j).wait_recv()
        pd[k] = spread(k, 1).astype(bf16)
        pa_copy(k).start()

    def back_far(k):
        pa_copy(k).wait_recv()
        zs[k - 1] = (spread(k, 0) + pa[k].astype(f32)).astype(bf16)
        pz_copy(k).start()

    def pass_on(u, k):
        z_copy(u, k).wait_recv()
        a_copy(u, k).start()

    def near_gather(u, k):
        a_copy(u, k).wait_recv()
        gather(u, k)

    near_gather(0, 0)
    pass_on(0, 1)
    near_gather(1, 0)
    near_gather(0, 1)
    expert(0)
    pass_on(0, 2)
    pass_on(0, 3)
    for k in (1, 2, 3):
        z_copy(1, k).start()
    expert(1)
    near_gather(0, 2)
    near_gather(0, 3)
    pass_on(1, 1)
    back_near(1)
    expert(2)
    back_far(1)
    expert(3)
    near_gather(1, 1)
    back_near(2)
    pass_on(1, 2)
    back_near(3)
    back_far(2)
    back_far(3)
    near_gather(1, 2)
    pass_on(1, 3)
    back_near(0)
    near_gather(1, 3)

    @pl.loop(0, width // 256)
    def _(n):
        cols = pl.ds(pl.multiple_of(n * 256, 256), 256)
        wd[:, cols] = jnp.dot(ht[...], gr[:, cols], preferred_element_type=f32).astype(bf16)

    store_down = pltpu.make_async_copy(wd, out_down, load_sem.at[2])
    store_down.start()

    pa_copy(0).wait_recv()
    total = spread(0, 0) + pa[0].astype(f32)
    for k in (1, 2, 3):
        pz_copy(k).wait_recv()
        total += zr[k - 1].astype(f32)
    out_tok[...] = total[:, :width].astype(bf16)
    terms = total[:, width:wide]
    lane8 = lax.broadcasted_iota(jnp.int32, out_gate.shape, 1)
    gates = jnp.zeros(out_gate.shape, f32)
    for r in range(ids_ref.shape[1]):
        term = jnp.sum(jnp.where(lane == ids_ref[:, r : r + 1], terms, 0.0), axis=1, keepdims=True)
        gates += jnp.where(lane8 == r, term, 0.0)
    out_gate[...] = gates.astype(bf16)

    for u in range(2):
        for k in range(4):
            if k:
                z_copy(u, k).wait_send()
            a_copy(u, k).wait_send()
            for j in (1, 2, 3):
                if k >= 2:
                    c_copy(u, k, j).wait_send()
                if u == 1:
                    c_copy(u, k, j).wait_recv()
    for k in range(4):
        rows = pl.ds(k * part, part)
        pa_copy(k).wait_send()
        if k:
            pz_copy(k).wait_send()
        if k >= 2:
            own_rows(k).wait()
            for j in (1, 2, 3):
                r_copy(k, j).wait_send()
        pltpu.make_async_copy(pg.at[rows], pre_hbm.at[rows], store_sem.at[4 + k]).wait()
        pltpu.make_async_copy(pu.at[rows], up_hbm.at[rows], store_sem.at[8 + k]).wait()
    store_down.wait()


def fused_body(
    tokens, grad_out, expert_ids, pair_slot, gate_weights,
    weight_gate, weight_up, weight_down, saved_gate, saved_up,
):
    f32, bf16 = jnp.float32, jnp.bfloat16
    tok, width = tokens.shape
    wide = width + EXT
    cap, hid_width = saved_gate.shape[1:]
    part = cap // 4
    four = part // 4
    pair = four // 2
    vmem, hbm = pl.BlockSpec(memory_space=pltpu.VMEM), pl.BlockSpec(memory_space=pl.ANY)
    dma = pltpu.SemaphoreType.DMA
    out_tok, out_gate, out_down, token_rows, pre, up = pl.pallas_call(
        fused_kernel,
        out_shape=[
            jax.ShapeDtypeStruct((tok, width), bf16),
            jax.ShapeDtypeStruct(expert_ids.shape, bf16),
            jax.ShapeDtypeStruct((hid_width, width), bf16),
            jax.ShapeDtypeStruct((cap, width), bf16),
            jax.ShapeDtypeStruct((cap, hid_width), bf16),
            jax.ShapeDtypeStruct((cap, hid_width), bf16),
        ],
        in_specs=[vmem] * 3 + [hbm] * 7,
        out_specs=[vmem] * 2 + [hbm] * 4,
        scratch_shapes=[
            pltpu.VMEM((4, 2, tok, wide), bf16),
            pltpu.VMEM((4, 2, tok, width), bf16),
            pltpu.VMEM((2, 3 * four, wide), bf16),
            pltpu.VMEM((2, 4 * four, width), bf16),
            pltpu.VMEM((cap, wide), bf16),
            pltpu.VMEM((2, 3 * four, wide), bf16),
            pltpu.VMEM((cap, wide), bf16),
            pltpu.VMEM((4, tok, wide), bf16),
            pltpu.VMEM((4, tok, wide), bf16),
            pltpu.VMEM((3, tok, wide), bf16),
            pltpu.VMEM((3, tok, wide), bf16),
            pltpu.VMEM((width, hid_width), bf16),
            pltpu.VMEM((width, hid_width), bf16),
            pltpu.VMEM((hid_width, width), bf16),
            pltpu.VMEM((cap, hid_width), bf16),
            pltpu.VMEM((cap, hid_width), bf16),
            pltpu.VMEM((part, hid_width), f32),
            pltpu.VMEM((hid_width, cap), bf16),
            pltpu.VMEM((8, 4 * pair, tok), bf16),
            pltpu.VMEM((8, tok, 4 * pair), bf16),
            pltpu.VMEM((4 * pair, EXT), bf16),
            dma((5,)), dma((8,)), dma((12,)),
            dma((9,)), dma((9,)), dma((12,)), dma((12,)),
            dma((24,)), dma((24,)), dma((12,)), dma((12,)),
        ],
        compiler_params=pltpu.CompilerParams(
            collective_id=0, has_side_effects=True, vmem_limit_bytes=60 * 1024 * 1024
        ),
        cost_estimate=pl.CostEstimate(
            flops=10 * cap * width * hid_width, bytes_accessed=20 * cap * width, transcendentals=0
        ),
    )(
        expert_ids, pair_slot, gate_weights, tokens, grad_out,
        weight_gate[0], weight_up[0], weight_down[0], saved_gate[0], saved_up[0],
    )
    gate_grad = lax.dot_general(token_rows, pre, OVER_ROWS, preferred_element_type=f32)
    up_grad = lax.dot_general(token_rows, up, OVER_ROWS, preferred_element_type=f32)
    return (
        out_tok, out_gate, gate_grad.astype(bf16)[None], up_grad.astype(bf16)[None], out_down[None]
    )


def body(*args):
    tokens, expert_ids, saved = args[0], args[2], args[8]
    if (
        (lax.axis_size("group"), lax.axis_size("member")) == (8, 4)
        and tokens.shape[0] % 128 == 0
        and tokens.shape[1] % 256 == 0
        and saved.shape[2] % 256 == 0
        and saved.shape[1] % 1536 == 0
    ):
        return fused_body(*args)
    return pair_body(*args)


def solution(mesh):
    flat, deep = P(AXES, None), P(AXES, None, None)
    return jax.shard_map(
        body,
        mesh=mesh,
        in_specs=(flat,) * 5 + (deep,) * 5,
        out_specs=(flat, flat, deep, deep, deep),
        check_vma=False,
    )
```

```python
import jax
import jax.numpy as jnp
from jax import lax
from jax.experimental import pallas as pl
from jax.experimental.pallas import tpu as pltpu
from jax.sharding import PartitionSpec as P

AXES = ("group", "member")


def expert_block(
    token_rows,
    grad_rows,
    route_gate,
    saved_pregate,
    saved_preup,
    weight_gate,
    weight_up,
    weight_down,
):
    pre_gate = saved_pregate.astype(jnp.float32)
    pre_up = saved_preup.astype(jnp.float32)
    gate_sigmoid = jax.nn.sigmoid(pre_gate)
    gate_swish = pre_gate * gate_sigmoid
    hidden = gate_swish * pre_up
    hidden_low = hidden.astype(jnp.bfloat16)
    route_scale = route_gate.astype(jnp.float32)[:, None]
    scaled_grads = (route_scale * grad_rows.astype(jnp.float32)).astype(jnp.bfloat16)
    over_rows = (((0,), (0,)), ((), ()))
    over_features = (((1,), (1,)), ((), ()))
    down_grad = lax.dot_general(
        hidden_low, scaled_grads, over_rows, preferred_element_type=jnp.float32
    )
    back_hidden = lax.dot_general(
        grad_rows, weight_down, over_features, preferred_element_type=jnp.float32
    )
    slot_gate = jnp.sum(hidden * back_hidden, axis=1).astype(jnp.bfloat16)
    hidden_grad = route_scale * back_hidden
    pregate_grad = (
        hidden_grad * pre_up * gate_sigmoid * (1.0 + pre_gate * (1.0 - gate_sigmoid))
    ).astype(jnp.bfloat16)
    preup_grad = (hidden_grad * gate_swish).astype(jnp.bfloat16)
    gate_grad = lax.dot_general(
        token_rows, pregate_grad, over_rows, preferred_element_type=jnp.float32
    )
    up_grad = lax.dot_general(token_rows, preup_grad, over_rows, preferred_element_type=jnp.float32)
    slot_grad = (
        lax.dot_general(
            pregate_grad, weight_gate, over_features, preferred_element_type=jnp.float32
        )
        + lax.dot_general(preup_grad, weight_up, over_features, preferred_element_type=jnp.float32)
    ).astype(jnp.bfloat16)
    return (slot_grad, slot_gate, gate_grad, up_grad, down_grad)


def pair_body(
    tokens,
    grad_out,
    expert_ids,
    pair_slot,
    gate_weights,
    weight_gate,
    weight_up,
    weight_down,
    saved_gate,
    saved_up,
):
    groups = lax.axis_size("group")
    members = lax.axis_size("member")
    experts = groups * members
    tok_rows, model_width = tokens.shape
    route_count = expert_ids.shape[1]
    capacity = saved_gate.shape[1]
    pair_rows = capacity // experts
    token_range = jnp.arange(tok_rows, dtype=jnp.int32)
    dest = (expert_ids * pair_rows + pair_slot).reshape(-1)
    slot_token = (
        jnp.full((experts * pair_rows,), tok_rows, jnp.int32)
        .at[dest]
        .set(jnp.repeat(token_range, route_count))
    )
    send_rows = jnp.take(tokens, slot_token, axis=0, mode="fill", fill_value=0)
    send_grads = jnp.take(grad_out, slot_token, axis=0, mode="fill", fill_value=0)
    send_gates = (
        jnp.zeros((experts * pair_rows,), jnp.bfloat16).at[dest].set(gate_weights.reshape(-1))
    )
    expert_rows, expert_grads, expert_gates = (
        lax.all_to_all(send_rows, ("group", "member"), split_axis=0, concat_axis=0, tiled=True),
        lax.all_to_all(send_grads, ("group", "member"), split_axis=0, concat_axis=0, tiled=True),
        lax.all_to_all(send_gates, ("group", "member"), split_axis=0, concat_axis=0, tiled=True),
    )
    slot_grad, slot_gate, gate_total, up_total, down_total = expert_block(
        expert_rows,
        expert_grads,
        expert_gates,
        saved_gate[0],
        saved_up[0],
        weight_gate[0],
        weight_up[0],
        weight_down[0],
    )
    back_rows, back_terms = (
        lax.all_to_all(slot_grad, ("group", "member"), split_axis=0, concat_axis=0, tiled=True),
        lax.all_to_all(slot_gate, ("group", "member"), split_axis=0, concat_axis=0, tiled=True),
    )
    per_route = jnp.take(back_rows, dest, axis=0).reshape(tok_rows, route_count, model_width)
    grad_tokens = jnp.sum(per_route.astype(jnp.float32), axis=1).astype(jnp.bfloat16)
    grad_gates = jnp.take(back_terms, dest, axis=0).reshape(tok_rows, route_count)
    return (
        grad_tokens,
        grad_gates,
        gate_total[None].astype(jnp.bfloat16),
        up_total[None].astype(jnp.bfloat16),
        down_total[None].astype(jnp.bfloat16),
    )


MESH_ID = pl.DeviceIdType.MESH
EXT = 128
OVER_LAST = (((1,), (1,)), ((), ()))


def fused_kernel(
    ids_ref, slots_ref, gates_ref, tok_hbm, grd_hbm, wg_hbm, wu_hbm, wd_hbm, sa_hbm, sb_hbm,
    out_tok, out_gate, out_wg, out_wu, out_wd, token_rows, last_pre, last_up,
    gd, td, gs, ts, gr, rs, rb, pd, pa, zs, zr, wg, wu, wd, pg, pu, bh, ht, pick_to, pick_from,
    sel, tile, load_sem, row_sem, store_sem, tile_sem,
    z_send, z_recv, a_send, a_recv, c_send, c_recv, r_send, r_recv,
):
    f32, bf16 = jnp.float32, jnp.bfloat16
    tok, width = tok_hbm.shape
    wide = width + EXT
    cap, hid_width = sa_hbm.shape
    part = cap // 4
    four = part // 4
    pair = four // 2
    g, z = lax.axis_index("group"), lax.axis_index("member")
    c, x, y = g % 2, (g // 2) % 2, g // 4
    a, b = x * (1 - c) + y * c, y * (1 - c) + x * c
    me = g * 4 + z
    near_z = z + 1 - 2 * (z % 2)
    inner = (z % 2 + z // 2) % 2

    def place(da, db, dc):
        pa_, pb_ = (1 - a if da else a), (1 - b if db else b)
        pc_ = 1 - c if dc else c
        px, py = pa_ * (1 - c) + pb_ * c, pb_ * (1 - c) + pa_ * c
        return (py * 2 + px) * 2 + pc_

    def plane(k):
        return (z, near_z, 2 - z // 2, 3 - 3 * (z // 2))[k]

    lane_to = ((0, 0, 0), (0, 0, 1), (0, 1, 0), (0, 1, 1))
    lane_from = ((0, 0, 0), (0, 0, 1), (0, 1, 0), (1, 0, 1))

    def source(j, i):
        return ((i, 0, 0), (0, i, 1), (i, 1, 0), (1, i, 1))[j]

    def remote(src, dst, ssem, rsem, group, member):
        return pltpu.make_async_remote_copy(
            src_ref=src, dst_ref=dst, send_sem=ssem, recv_sem=rsem,
            device_id=(group, member), device_id_type=MESH_ID,
        )

    dense = (gd, td)

    hops = ((0, 1, True), (0, 2, False), (1, 3, False), (2, 2, True), (3, 3, True))

    def z_copy(u, n):
        here, there, outward = hops[n]
        src, dst = (gd.at[here, 0], gd.at[there, 0]) if u == 0 else (td.at[here], td.at[there])
        return remote(
            src, dst, z_send.at[u * 5 + n], z_recv.at[u * 3 + there - 1], g,
            near_z if outward else 3 - z,
        )

    def z_arrived(u, k):
        z_copy(u, k - 1).wait_recv()

    def if_inner(act):
        @pl.when(inner == 1)
        def _():
            act()

    def a_copy(u, k):
        n = u * 4 + k
        return remote(
            dense[u].at[k, 0], dense[u].at[k, 1], a_send.at[n], a_recv.at[n], place(1, 0, 0), z
        )

    def c_copy(u, k, j):
        n = (u * 4 + k) * 3 + j - 1
        src, dst = (gs, gr) if u == 0 else (ts, token_rows)
        return remote(
            src.at[k % 2, pl.ds((j - 1) * four, four)], dst.at[pl.ds(k * part + j * four, four)],
            c_send.at[n], c_recv.at[n], place(*lane_to[j]), z,
        )

    def r_copy(k, j):
        n = k * 3 + j - 1
        return remote(
            rs.at[k, pl.ds((j - 1) * four, four)], rb.at[pl.ds(k * part + j * four, four)],
            r_send.at[n], r_recv.at[n], place(*lane_from[j]), z,
        )

    def pa_copy(k):
        return remote(pd.at[k], pa.at[k], a_send.at[5 + k], a_recv.at[5 + k], place(1, 0, 0), z)

    def pz_copy(k):
        there = 0 if k == 1 else 2 - inner
        return remote(
            zs.at[k - 1], zr.at[there], z_send.at[9 + k], z_recv.at[6 + there], g, plane(k)
        )

    def pz_arrived(k):
        remote(zs.at[k - 1], zr.at[k - 1], z_send.at[9 + k], z_recv.at[5 + k], g, plane(k)).wait_recv()

    def own_rows(k):
        return pltpu.make_async_copy(
            ts.at[k % 2, pl.ds(3 * four, four)], token_rows.at[pl.ds(k * part, four)],
            store_sem.at[k],
        )

    load_grd = pltpu.make_async_copy(grd_hbm, gd.at[0, 0, :, pl.ds(0, width)], load_sem.at[0])
    load_tok = pltpu.make_async_copy(tok_hbm, td.at[0, 0], load_sem.at[1])
    load_wd = pltpu.make_async_copy(wd_hbm, wd, load_sem.at[2])
    load_wg = pltpu.make_async_copy(wg_hbm, wg, load_sem.at[3])
    load_wu = pltpu.make_async_copy(wu_hbm, wu, load_sem.at[4])
    load_grd.start()
    load_tok.start()

    barrier = pltpu.get_barrier_semaphore()
    peers = [(place(*p), z) for p in ((1, 0, 0), (1, 0, 1), (0, 1, 0), (0, 1, 1), (0, 0, 1))]
    peers += [(g, plane(k)) for k in (1, 2, 3)]
    for peer in peers:
        pl.semaphore_signal(barrier, inc=1, device_id=peer, device_id_type=MESH_ID)

    line = lax.broadcasted_iota(jnp.int32, (EXT, tok), 0)
    ext = jnp.zeros((EXT, tok), f32)
    for r in range(ids_ref.shape[0]):
        expert_at = ids_ref[r : r + 1, :]
        ext += jnp.where(line == expert_at, gates_ref[r : r + 1, :].astype(f32), 0.0)
        ext += jnp.where(line == expert_at + 32, (slots_ref[r : r + 1, :] + 1).astype(f32), 0.0)
    gd[0, 0, :, width:wide] = ext.T.astype(bf16)
    lane_pair = lax.broadcasted_iota(jnp.int32, (pair, EXT), 1)
    for j in range(4):
        expert = place(*lane_to[j]) * 4 + z
        sel[j * pair : (j + 1) * pair, :] = jnp.where(lane_pair == expert + 32, 1.0, 0.0).astype(bf16)

    def z_first(u):
        z_copy(u, 0).start()
        if_inner(z_copy(u, 1).start)

    pl.semaphore_wait(barrier, len(peers))
    load_grd.wait()
    z_first(0)
    a_copy(0, 0).start()
    load_tok.wait()
    a_copy(1, 0).start()
    load_wd.start()
    load_wg.start()
    load_wu.start()
    for k in range(4):
        for j in range(4):
            for i in range(2):
                row = (place(*source(j, i)) * 4 + plane(k)) * pair
                row = pl.ds(pl.multiple_of(row, 16), pair)
                at = pl.ds(k * part + j * four + i * pair, pair)
                pltpu.make_async_copy(sa_hbm.at[row], pg.at[at], row_sem.at[k]).start()
                pltpu.make_async_copy(sb_hbm.at[row], pu.at[at], row_sem.at[4 + k]).start()

    def want(shape, dim):
        at = lax.broadcasted_iota(jnp.int32, shape, dim)
        for _ in range(3):
            at = jnp.where(at >= pair, at - pair, at)
        return (at + 1).astype(f32)

    def gather(u, k):
        if u == 1 and k >= 2:
            own_rows(k - 2).wait()
        if k >= 2:
            for j in (1, 2, 3):
                c_copy(u, k - 2, j).wait_send()
        for i in range(2):
            if u == 0:
                tags = gd[k, i, :, width:wide]
                slot_at = lax.dot_general(sel[...], tags, OVER_LAST, preferred_element_type=f32)
                pick_to[k * 2 + i] = (slot_at == want((4 * pair, tok), 0)).astype(bf16)
                slot_at = lax.dot_general(tags, sel[...], OVER_LAST, preferred_element_type=f32)
                pick_from[k * 2 + i] = (slot_at == want((tok, 4 * pair), 1)).astype(bf16)
            got = jnp.dot(
                pick_to[k * 2 + i], dense[u][k, i], preferred_element_type=f32
            ).astype(bf16)
            if u == 0:
                gr[pl.ds(k * part + i * pair, pair), :] = got[:pair]
            else:
                ts[k % 2, pl.ds(3 * four + i * pair, pair), :] = got[:pair]
            send = gs if u == 0 else ts
            for j in (1, 2, 3):
                send[k % 2, pl.ds((j - 1) * four + i * pair, pair), :] = got[
                    j * pair : (j + 1) * pair
                ]
        for j in (1, 2, 3):
            c_copy(u, k, j).start()
        if u == 1:
            own_rows(k).start()

    def expert(k):
        rows = pl.ds(k * part, part)
        for j in (1, 2, 3):
            c_copy(0, k, j).wait_recv()
        if k == 0:
            load_wd.wait()
            load_wg.wait()
            load_wu.wait()
        pltpu.make_async_copy(sa_hbm.at[pl.ds(0, part)], pg.at[rows], row_sem.at[k]).wait()
        pltpu.make_async_copy(sb_hbm.at[pl.ds(0, part)], pu.at[rows], row_sem.at[4 + k]).wait()

        @pl.loop(0, hid_width // 256)
        def _(n):
            cols = pl.ds(pl.multiple_of(n * 256, 256), 256)
            bh[:, cols] = lax.dot_general(
                gr[rows, :width], wd[cols, :], OVER_LAST, preferred_element_type=f32
            )

        def hidden_rows(j, put):
            at = k * part + j * four
            here = pl.ds(at if isinstance(j, int) else pl.multiple_of(at, 16), four)
            there = pl.ds(j * four if isinstance(j, int) else pl.multiple_of(j * four, 16), four)
            tag = lax.broadcasted_iota(jnp.int32, (four, EXT), 1) == me
            route = jnp.sum(
                jnp.where(tag, gr[here, width:wide].astype(f32), 0.0), axis=1, keepdims=True
            )
            pre, up, back = pg[here, :].astype(f32), pu[here, :].astype(f32), bh[there, :]
            sig = jax.nn.sigmoid(pre)
            swish = pre * sig
            hidden = swish * up
            term = jnp.sum(hidden * back, axis=1, keepdims=True)
            back = route * back
            pg[here, :] = (back * up * sig * (1.0 + pre * (1.0 - sig))).astype(bf16)
            pu[here, :] = (back * swish).astype(bf16)
            bh[there, :] = hidden
            put(jnp.where(tag, term, 0.0).astype(bf16))
            gr[here, :width] = (route * gr[here, :width].astype(f32)).astype(bf16)

        def put_own(value):
            rb[pl.ds(k * part, four), width:wide] = value

        hidden_rows(0, put_own)

        @pl.loop(1, 4)
        def _(j):
            def put_far(value):
                rs[k, pl.ds(pl.multiple_of((j - 1) * four, 16), four), width:wide] = value

            hidden_rows(j, put_far)

        @pl.loop(0, width // 256)
        def _(n):
            cols = pl.ds(pl.multiple_of(n * 256, 256), 256)
            back = lax.dot_general(
                pg[rows, :], wg[cols, :], OVER_LAST, preferred_element_type=f32
            ) + lax.dot_general(pu[rows, :], wu[cols, :], OVER_LAST, preferred_element_type=f32)
            back = back.astype(bf16)
            rb[pl.ds(k * part, four), cols] = back[:four]
            rs[k, :, cols] = back[four:]

        for j in (1, 2, 3):
            r_copy(k, j).start()
        if k == 3:
            pltpu.make_async_copy(pg.at[rows], last_pre, store_sem.at[4]).start()
            pltpu.make_async_copy(pu.at[rows], last_up, store_sem.at[5]).start()
        ht[:, rows] = bh[...].astype(bf16).T

    def spread(k, i):
        got = jnp.concatenate(
            [rb[pl.ds(k * part + j * four + i * pair, pair), :] for j in range(4)], axis=0
        )
        return jnp.dot(pick_from[k * 2 + i], got, preferred_element_type=f32)

    def back_near(k):
        for j in (1, 2, 3):
            r_copy(k, j).wait_recv()
        pd[k] = spread(k, 1).astype(bf16)
        pa_copy(k).start()

    def back_far(k):
        pa_copy(k).wait_recv()
        zs[k - 1] = (spread(k, 0) + pa[k].astype(f32)).astype(bf16)
        pz_copy(k).start()

    def forward(u, k):
        z_arrived(u, k)
        if_inner(z_copy(u, k + 1).start)

    def to_neighbour(k):
        a_copy(0, k).start()

    def gather_grads(k):
        a_copy(0, k).wait_recv()
        gather(0, k)

    def gather_tokens(k):
        gather(1, k)

    def tokens_along_z():
        a_copy(1, 0).wait_recv()
        z_first(1)

    def weight_down_grad():
        @pl.loop(0, width // 256)
        def _(n):
            cols = pl.ds(pl.multiple_of(n * 256, 256), 256)
            wd[:, cols] = jnp.dot(ht[...], gr[:, cols], preferred_element_type=f32).astype(bf16)

        pltpu.make_async_copy(wd, out_wd, load_sem.at[2]).start()

    def tile_copy(n, slot):
        cols = pl.ds(pl.multiple_of(n * 256, 256), 256)
        return pltpu.make_async_copy(token_rows.at[pl.ds(0, 3 * part), cols], tile.at[slot], tile_sem.at[slot])

    def weight_in_grads():
        for k in range(3):
            for j in (1, 2, 3):
                c_copy(1, k, j).wait_recv()
        own_rows(2).wait()
        first = pl.ds(0, 3 * part)
        count = width // 256
        tile_copy(0, 0).start()

        @pl.loop(0, count)
        def _(n):
            slot = n % 2

            @pl.when(n + 1 < count)
            def _():
                tile_copy(n + 1, 1 - slot).start()

            tile_copy(n, slot).wait()
            rows = pl.ds(pl.multiple_of(n * 256, 256), 256)
            flipped = tile[slot].T
            wg[rows, :] = jnp.dot(flipped, pg[first, :], preferred_element_type=f32).astype(bf16)
            wu[rows, :] = jnp.dot(flipped, pu[first, :], preferred_element_type=f32).astype(bf16)

        pltpu.make_async_copy(wg, out_wg, load_sem.at[3]).start()
        pltpu.make_async_copy(wu, out_wu, load_sem.at[4]).start()

    def finish():
        pa_copy(0).wait_recv()
        total = spread(0, 0) + pa[0].astype(f32)
        for k in (1, 2, 3):
            pz_arrived(k)
            total += zr[k - 1].astype(f32)
        out_tok[...] = total[:, :width].astype(bf16)
        terms = total[:, width:wide].T
        row8 = lax.broadcasted_iota(jnp.int32, out_gate.shape, 0)
        gates = jnp.zeros(out_gate.shape, f32)
        for r in range(ids_ref.shape[0]):
            term = jnp.where(line == ids_ref[r : r + 1, :], terms, 0.0)
            gates += jnp.where(row8 == r, jnp.sum(term, axis=0, keepdims=True), 0.0)
        out_gate[...] = gates.astype(bf16)

    gather_grads(0)
    forward(0, 1)
    to_neighbour(1)
    forward(0, 2)
    to_neighbour(2)
    gather_grads(1)
    forward(0, 3)
    gather_grads(2)
    tokens_along_z()
    to_neighbour(3)
    expert(0)
    gather_grads(3)
    expert(1)
    forward(1, 1)
    expert(2)
    gather_tokens(0)
    forward(1, 2)
    expert(3)
    back_near(2)
    back_near(1)
    forward(1, 3)
    gather_tokens(1)
    back_far(2)
    back_near(3)
    back_far(1)
    gather_tokens(2)
    gather_tokens(3)
    back_far(3)
    weight_down_grad()
    back_near(0)
    weight_in_grads()
    finish()

    for u in range(2):
        z_copy(u, 0).wait_send()
        for n in range(1, 5):
            if_inner(z_copy(u, n).wait_send)
        for k in (2, 3):
            for j in (1, 2, 3):
                c_copy(u, k, j).wait_send()
    for j in (1, 2, 3):
        c_copy(1, 3, j).wait_recv()
    own_rows(3).wait()
    a_copy(1, 0).wait_send()
    for k in range(4):
        a_copy(0, k).wait_send()
        pa_copy(k).wait_send()
        if k:
            pz_copy(k).wait_send()
        for j in (1, 2, 3):
            r_copy(k, j).wait_send()
    rows = pl.ds(3 * part, part)
    pltpu.make_async_copy(pg.at[rows], last_pre, store_sem.at[4]).wait()
    pltpu.make_async_copy(pu.at[rows], last_up, store_sem.at[5]).wait()
    pltpu.make_async_copy(wd, out_wd, load_sem.at[2]).wait()
    pltpu.make_async_copy(wg, out_wg, load_sem.at[3]).wait()
    pltpu.make_async_copy(wu, out_wu, load_sem.at[4]).wait()


def last_kernel(
    tok_ref, gate_ref, wg_ref, wu_ref, wd_ref, rows_ref, pre_ref, up_ref,
    out_tok, out_gate, out_wg, out_wu, out_wd,
):
    f32, bf16 = jnp.float32, jnp.bfloat16
    flipped = rows_ref[...].T
    for ref, into, part in ((pre_ref, out_wg, wg_ref), (up_ref, out_wu, wu_ref)):
        got = jnp.dot(flipped, ref[...], preferred_element_type=f32)
        into[...] = (got + part[...].astype(f32)).astype(bf16)
    out_tok[...] = tok_ref[...]
    out_gate[...] = gate_ref[...]
    out_wd[...] = wd_ref[...]


def last_part(out_tok, out_gate, out_wg, out_wu, out_wd, rows, pre, up):
    tok, width = out_tok.shape
    part, hid_width = pre.shape
    steps = width // 256
    start = rows.shape[0] // part - 1

    def down(count, columns):
        return pl.BlockSpec((count, columns), lambda n: (n, 0))

    def whole(a):
        return pl.BlockSpec(a.shape, lambda n: (0, 0))

    parts = [
        down(tok // steps, width), whole(out_gate), down(256, hid_width), down(256, hid_width),
        down(hid_width // steps, width),
    ]
    outs = (out_tok, out_gate, out_wg, out_wu, out_wd)
    return pl.pallas_call(
        last_kernel,
        grid=(steps,),
        out_shape=[jax.ShapeDtypeStruct(a.shape, a.dtype) for a in outs],
        in_specs=parts + [
            pl.BlockSpec((part, 256), lambda n: (start, n)), whole(pre), whole(up)
        ],
        out_specs=parts,
        compiler_params=pltpu.CompilerParams(vmem_limit_bytes=62 * 1024 * 1024),
    )(*outs, rows, pre, up)


def fused_body(
    tokens, grad_out, expert_ids, pair_slot, gate_weights,
    weight_gate, weight_up, weight_down, saved_gate, saved_up,
):
    f32, bf16 = jnp.float32, jnp.bfloat16
    tok, width = tokens.shape
    wide = width + EXT
    cap, hid_width = saved_gate.shape[1:]
    part = cap // 4
    four = part // 4
    pair = four // 2
    vmem, hbm = pl.BlockSpec(memory_space=pltpu.VMEM), pl.BlockSpec(memory_space=pl.ANY)
    dma = pltpu.SemaphoreType.DMA
    outs = pl.pallas_call(
        fused_kernel,
        out_shape=[
            jax.ShapeDtypeStruct((tok, width), bf16),
            jax.ShapeDtypeStruct(expert_ids.shape[::-1], bf16),
            jax.ShapeDtypeStruct((width, hid_width), bf16),
            jax.ShapeDtypeStruct((width, hid_width), bf16),
            jax.ShapeDtypeStruct((hid_width, width), bf16),
            jax.ShapeDtypeStruct((cap, width), bf16),
            jax.ShapeDtypeStruct((part, hid_width), bf16),
            jax.ShapeDtypeStruct((part, hid_width), bf16),
        ],
        in_specs=[vmem] * 3 + [hbm] * 7,
        out_specs=[vmem] * 2 + [hbm] * 6,
        scratch_shapes=[
            pltpu.VMEM((4, 2, tok, wide), bf16),
            pltpu.VMEM((4, 2, tok, width), bf16),
            pltpu.VMEM((2, 3 * four, wide), bf16),
            pltpu.VMEM((2, 4 * four, width), bf16),
            pltpu.VMEM((cap, wide), bf16),
            pltpu.VMEM((4, 3 * four, wide), bf16),
            pltpu.VMEM((cap, wide), bf16),
            pltpu.VMEM((4, tok, wide), bf16),
            pltpu.VMEM((4, tok, wide), bf16),
            pltpu.VMEM((3, tok, wide), bf16),
            pltpu.VMEM((3, tok, wide), bf16),
            pltpu.VMEM((width, hid_width), bf16),
            pltpu.VMEM((width, hid_width), bf16),
            pltpu.VMEM((hid_width, width), bf16),
            pltpu.VMEM((cap, hid_width), bf16),
            pltpu.VMEM((cap, hid_width), bf16),
            pltpu.VMEM((part, hid_width), f32),
            pltpu.VMEM((hid_width, cap), bf16),
            pltpu.VMEM((8, 4 * pair, tok), bf16),
            pltpu.VMEM((8, tok, 4 * pair), bf16),
            pltpu.VMEM((4 * pair, EXT), bf16),
            pltpu.VMEM((2, 3 * part, 256), bf16),
            dma((5,)), dma((8,)), dma((6,)), dma((2,)),
            dma((13,)), dma((9,)), dma((9,)), dma((9,)),
            dma((24,)), dma((24,)), dma((12,)), dma((12,)),
        ],
        compiler_params=pltpu.CompilerParams(
            collective_id=0, has_side_effects=True, vmem_limit_bytes=62 * 1024 * 1024
        ),
        cost_estimate=pl.CostEstimate(
            flops=10 * cap * width * hid_width, bytes_accessed=20 * cap * width, transcendentals=0
        ),
    )(
        expert_ids.T, pair_slot.T, gate_weights.T, tokens, grad_out,
        weight_gate[0], weight_up[0], weight_down[0], saved_gate[0], saved_up[0],
    )
    out_tok, out_gate, out_wg, out_wu, out_wd = last_part(*outs)
    return (out_tok, out_gate.T, out_wg[None], out_wu[None], out_wd[None])


def body(*args):
    tokens, saved = args[0], args[8]
    if (
        (lax.axis_size("group"), lax.axis_size("member")) == (8, 4)
        and tokens.shape[0] % 128 == 0
        and tokens.shape[1] % 256 == 0
        and saved.shape[2] % 256 == 0
        and saved.shape[1] % 1536 == 0
    ):
        return fused_body(*args)
    return pair_body(*args)


def solution(mesh):
    flat, deep = P(AXES, None), P(AXES, None, None)
    return jax.shard_map(
        body,
        mesh=mesh,
        in_specs=(flat,) * 5 + (deep,) * 5,
        out_specs=(flat, flat, deep, deep, deep),
        check_vma=False,
    )
```

```python
import jax
import jax.numpy as jnp
from jax import lax
from jax.experimental import pallas as pl
from jax.experimental.pallas import tpu as pltpu
from jax.sharding import PartitionSpec as P

AXES = ("group", "member")


def expert_block(
    token_rows,
    grad_rows,
    route_gate,
    saved_pregate,
    saved_preup,
    weight_gate,
    weight_up,
    weight_down,
):
    pre_gate = saved_pregate.astype(jnp.float32)
    pre_up = saved_preup.astype(jnp.float32)
    gate_sigmoid = jax.nn.sigmoid(pre_gate)
    gate_swish = pre_gate * gate_sigmoid
    hidden = gate_swish * pre_up
    hidden_low = hidden.astype(jnp.bfloat16)
    route_scale = route_gate.astype(jnp.float32)[:, None]
    scaled_grads = (route_scale * grad_rows.astype(jnp.float32)).astype(jnp.bfloat16)
    over_rows = (((0,), (0,)), ((), ()))
    over_features = (((1,), (1,)), ((), ()))
    down_grad = lax.dot_general(
        hidden_low, scaled_grads, over_rows, preferred_element_type=jnp.float32
    )
    back_hidden = lax.dot_general(
        grad_rows, weight_down, over_features, preferred_element_type=jnp.float32
    )
    slot_gate = jnp.sum(hidden * back_hidden, axis=1).astype(jnp.bfloat16)
    hidden_grad = route_scale * back_hidden
    pregate_grad = (
        hidden_grad * pre_up * gate_sigmoid * (1.0 + pre_gate * (1.0 - gate_sigmoid))
    ).astype(jnp.bfloat16)
    preup_grad = (hidden_grad * gate_swish).astype(jnp.bfloat16)
    gate_grad = lax.dot_general(
        token_rows, pregate_grad, over_rows, preferred_element_type=jnp.float32
    )
    up_grad = lax.dot_general(token_rows, preup_grad, over_rows, preferred_element_type=jnp.float32)
    slot_grad = (
        lax.dot_general(
            pregate_grad, weight_gate, over_features, preferred_element_type=jnp.float32
        )
        + lax.dot_general(preup_grad, weight_up, over_features, preferred_element_type=jnp.float32)
    ).astype(jnp.bfloat16)
    return (slot_grad, slot_gate, gate_grad, up_grad, down_grad)


def pair_body(
    tokens,
    grad_out,
    expert_ids,
    pair_slot,
    gate_weights,
    weight_gate,
    weight_up,
    weight_down,
    saved_gate,
    saved_up,
):
    groups = lax.axis_size("group")
    members = lax.axis_size("member")
    experts = groups * members
    tok_rows, model_width = tokens.shape
    route_count = expert_ids.shape[1]
    capacity = saved_gate.shape[1]
    pair_rows = capacity // experts
    token_range = jnp.arange(tok_rows, dtype=jnp.int32)
    dest = (expert_ids * pair_rows + pair_slot).reshape(-1)
    slot_token = (
        jnp.full((experts * pair_rows,), tok_rows, jnp.int32)
        .at[dest]
        .set(jnp.repeat(token_range, route_count))
    )
    send_rows = jnp.take(tokens, slot_token, axis=0, mode="fill", fill_value=0)
    send_grads = jnp.take(grad_out, slot_token, axis=0, mode="fill", fill_value=0)
    send_gates = (
        jnp.zeros((experts * pair_rows,), jnp.bfloat16).at[dest].set(gate_weights.reshape(-1))
    )
    expert_rows, expert_grads, expert_gates = (
        lax.all_to_all(send_rows, ("group", "member"), split_axis=0, concat_axis=0, tiled=True),
        lax.all_to_all(send_grads, ("group", "member"), split_axis=0, concat_axis=0, tiled=True),
        lax.all_to_all(send_gates, ("group", "member"), split_axis=0, concat_axis=0, tiled=True),
    )
    slot_grad, slot_gate, gate_total, up_total, down_total = expert_block(
        expert_rows,
        expert_grads,
        expert_gates,
        saved_gate[0],
        saved_up[0],
        weight_gate[0],
        weight_up[0],
        weight_down[0],
    )
    back_rows, back_terms = (
        lax.all_to_all(slot_grad, ("group", "member"), split_axis=0, concat_axis=0, tiled=True),
        lax.all_to_all(slot_gate, ("group", "member"), split_axis=0, concat_axis=0, tiled=True),
    )
    per_route = jnp.take(back_rows, dest, axis=0).reshape(tok_rows, route_count, model_width)
    grad_tokens = jnp.sum(per_route.astype(jnp.float32), axis=1).astype(jnp.bfloat16)
    grad_gates = jnp.take(back_terms, dest, axis=0).reshape(tok_rows, route_count)
    return (
        grad_tokens,
        grad_gates,
        gate_total[None].astype(jnp.bfloat16),
        up_total[None].astype(jnp.bfloat16),
        down_total[None].astype(jnp.bfloat16),
    )


MESH_ID = pl.DeviceIdType.MESH
EXT = 128
OVER_LAST = (((1,), (1,)), ((), ()))


def fused_kernel(
    ids_ref, slots_ref, gates_ref, tok_hbm, grd_hbm, wg_hbm, wu_hbm, wd_hbm, sa_hbm, sb_hbm,
    out_tok, out_gate, out_wg, out_wu, out_wd, token_rows, last_pre, last_up,
    gd, td, gs, ts, gr, rs, rb, pd, pa, zs, zr, wg, wu, wd, pg, pu, bh, ht, pick_to, pick_from,
    sel, sel_gate, tile, load_sem, row_sem, store_sem, tile_sem,
    z_send, z_recv, a_send, a_recv, c_send, c_recv, r_send, r_recv,
):
    f32, bf16 = jnp.float32, jnp.bfloat16
    tok, width = tok_hbm.shape
    wide = width + EXT
    cap, hid_width = sa_hbm.shape
    part = cap // 4
    four = part // 4
    pair = four // 2
    g, z = lax.axis_index("group"), lax.axis_index("member")
    c, x, y = g % 2, (g // 2) % 2, g // 4
    a, b = x * (1 - c) + y * c, y * (1 - c) + x * c
    me = g * 4 + z
    near_z = z + 1 - 2 * (z % 2)
    inner = (z % 2 + z // 2) % 2

    def place(da, db, dc):
        pa_, pb_ = (1 - a if da else a), (1 - b if db else b)
        pc_ = 1 - c if dc else c
        px, py = pa_ * (1 - c) + pb_ * c, pb_ * (1 - c) + pa_ * c
        return (py * 2 + px) * 2 + pc_

    def plane(k):
        return (z, near_z, 2 - z // 2, 3 - 3 * (z // 2))[k]

    lane_to = ((0, 0, 0), (0, 0, 1), (0, 1, 0), (0, 1, 1))
    lane_from = ((0, 0, 0), (0, 0, 1), (0, 1, 0), (1, 0, 1))

    def source(j, i):
        return ((i, 0, 0), (0, i, 1), (i, 1, 0), (1, i, 1))[j]

    def remote(src, dst, ssem, rsem, group, member):
        return pltpu.make_async_remote_copy(
            src_ref=src, dst_ref=dst, send_sem=ssem, recv_sem=rsem,
            device_id=(group, member), device_id_type=MESH_ID,
        )

    dense = (gd, td)

    hops = ((0, 1, True), (0, 2, False), (1, 3, False), (2, 2, True), (3, 3, True))

    def z_copy(u, n):
        here, there, outward = hops[n]
        src, dst = (gd.at[here, 0], gd.at[there, 0]) if u == 0 else (td.at[here], td.at[there])
        return remote(
            src, dst, z_send.at[u * 5 + n], z_recv.at[u * 3 + there - 1], g,
            near_z if outward else 3 - z,
        )

    def z_arrived(u, k):
        z_copy(u, k - 1).wait_recv()

    def if_inner(act):
        @pl.when(inner == 1)
        def _():
            act()

    def a_copy(u, k):
        n = u * 4 + k
        return remote(
            dense[u].at[k, 0], dense[u].at[k, 1], a_send.at[n], a_recv.at[n], place(1, 0, 0), z
        )

    def c_copy(u, k, j):
        n = (u * 4 + k) * 3 + j - 1
        src, dst = (gs, gr) if u == 0 else (ts, token_rows)
        return remote(
            src.at[k % 2, pl.ds((j - 1) * four, four)], dst.at[pl.ds(k * part + j * four, four)],
            c_send.at[n], c_recv.at[n], place(*lane_to[j]), z,
        )

    def r_copy(k, j):
        n = k * 3 + j - 1
        return remote(
            rs.at[k, pl.ds((j - 1) * four, four)], rb.at[pl.ds(k * part + j * four, four)],
            r_send.at[n], r_recv.at[n], place(*lane_from[j]), z,
        )

    def pa_copy(k):
        return remote(pd.at[k], pa.at[k], a_send.at[5 + k], a_recv.at[5 + k], place(1, 0, 0), z)

    def pz_copy(k):
        if k == 1:
            two = pl.ds(0, 2)
            return remote(zs.at[two], zr.at[two], z_send.at[10], z_recv.at[6], g, near_z)
        there = 3 - inner
        return remote(zs.at[k], zr.at[there], z_send.at[9 + k], z_recv.at[5 + there], g, plane(k))

    def pz_arrived(k):
        remote(zs.at[k], zr.at[k], z_send.at[9 + k], z_recv.at[5 + k], g, plane(k)).wait_recv()

    def own_rows(k):
        return pltpu.make_async_copy(
            ts.at[k % 2, pl.ds(3 * four, four)], token_rows.at[pl.ds(k * part, four)],
            store_sem.at[k],
        )

    load_grd = pltpu.make_async_copy(grd_hbm, gd.at[0, 0, :, pl.ds(0, width)], load_sem.at[0])
    load_tok = pltpu.make_async_copy(tok_hbm, td.at[0, 0], load_sem.at[1])
    load_wd = pltpu.make_async_copy(wd_hbm, wd, load_sem.at[2])
    load_wg = pltpu.make_async_copy(wg_hbm, wg, load_sem.at[3])
    load_wu = pltpu.make_async_copy(wu_hbm, wu, load_sem.at[4])
    load_grd.start()
    load_tok.start()

    barrier = pltpu.get_barrier_semaphore()
    peers = [(place(*p), z) for p in ((1, 0, 0), (1, 0, 1), (0, 1, 0), (0, 1, 1), (0, 0, 1))]
    peers += [(g, plane(k)) for k in (1, 2, 3)]
    for peer in peers:
        pl.semaphore_signal(barrier, inc=1, device_id=peer, device_id_type=MESH_ID)

    line = lax.broadcasted_iota(jnp.int32, (EXT, tok), 0)
    ext = jnp.zeros((EXT, tok), f32)
    for r in range(ids_ref.shape[0]):
        expert_at = ids_ref[r : r + 1, :]
        ext += jnp.where(line == expert_at, gates_ref[r : r + 1, :].astype(f32), 0.0)
        ext += jnp.where(line == expert_at + 32, (slots_ref[r : r + 1, :] + 1).astype(f32), 0.0)
    gd[0, 0, :, width:wide] = ext.T.astype(bf16)
    lane_pair = lax.broadcasted_iota(jnp.int32, (pair, EXT), 1)
    for j in range(4):
        expert_at = place(*lane_to[j]) * 4 + z
        at = pl.ds(j * pair, pair)
        sel[at, :] = jnp.where(lane_pair == expert_at + 32, 1.0, 0.0).astype(bf16)
        sel_gate[at, :] = jnp.where(lane_pair == expert_at, 1.0, 0.0).astype(bf16)

    def z_first(u):
        z_copy(u, 0).start()
        if_inner(z_copy(u, 1).start)

    pl.semaphore_wait(barrier, len(peers))
    load_grd.wait()
    z_first(0)
    a_copy(0, 0).start()
    load_tok.wait()
    a_copy(1, 0).start()
    load_wd.start()
    load_wg.start()
    load_wu.start()
    for k in range(4):
        for j in range(4):
            for i in range(2):
                row = (place(*source(j, i)) * 4 + plane(k)) * pair
                row = pl.ds(pl.multiple_of(row, 16), pair)
                at = pl.ds(k * part + j * four + i * pair, pair)
                pltpu.make_async_copy(sa_hbm.at[row], pg.at[at], row_sem.at[k]).start()
                pltpu.make_async_copy(sb_hbm.at[row], pu.at[at], row_sem.at[4 + k]).start()

    def want(shape, dim):
        at = lax.broadcasted_iota(jnp.int32, shape, dim)
        for _ in range(3):
            at = jnp.where(at >= pair, at - pair, at)
        return (at + 1).astype(f32)

    def gather(u, k):
        if u == 1 and k >= 2:
            own_rows(k - 2).wait()
        if k >= 2:
            for j in (1, 2, 3):
                c_copy(u, k - 2, j).wait_send()
        for i in range(2):
            if u == 0:
                tags = gd[k, i, :, width:wide]
                slot_at = lax.dot_general(sel[...], tags, OVER_LAST, preferred_element_type=f32)
                gate_at = lax.dot_general(sel_gate[...], tags, OVER_LAST, preferred_element_type=f32)
                hit = slot_at == want((4 * pair, tok), 0)
                pick_to[k * 2 + i] = jnp.where(hit, 1.0, 0.0).astype(bf16)
                pick = jnp.where(hit, gate_at, 0.0).astype(bf16)
                slot_at = lax.dot_general(tags, sel[...], OVER_LAST, preferred_element_type=f32)
                pick_from[k * 2 + i] = (slot_at == want((tok, 4 * pair), 1)).astype(bf16)
            if u == 0:
                got = jnp.dot(pick, gd[k, i, :, :width], preferred_element_type=f32)
            else:
                got = jnp.dot(pick_to[k * 2 + i], td[k, i], preferred_element_type=f32)
            got = got.astype(bf16)
            if u == 0:
                gr[pl.ds(k * part + i * pair, pair), :] = got[:pair]
            else:
                ts[k % 2, pl.ds(3 * four + i * pair, pair), :] = got[:pair]
            send = gs if u == 0 else ts
            for j in (1, 2, 3):
                send[k % 2, pl.ds((j - 1) * four + i * pair, pair), :] = got[
                    j * pair : (j + 1) * pair
                ]
        for j in (1, 2, 3):
            c_copy(u, k, j).start()
        if u == 1:
            own_rows(k).start()

    def expert(k):
        rows = pl.ds(k * part, part)
        for j in (1, 2, 3):
            c_copy(0, k, j).wait_recv()
        if k == 0:
            load_wd.wait()
            load_wg.wait()
            load_wu.wait()
        pltpu.make_async_copy(sa_hbm.at[pl.ds(0, part)], pg.at[rows], row_sem.at[k]).wait()
        pltpu.make_async_copy(sb_hbm.at[pl.ds(0, part)], pu.at[rows], row_sem.at[4 + k]).wait()

        @pl.loop(0, hid_width // 256)
        def _(n):
            cols = pl.ds(pl.multiple_of(n * 256, 256), 256)
            bh[:, cols] = lax.dot_general(
                gr[rows, :], wd[cols, :], OVER_LAST, preferred_element_type=f32
            )

        def hidden_rows(j, put):
            at = k * part + j * four
            here = pl.ds(at if isinstance(j, int) else pl.multiple_of(at, 16), four)
            there = pl.ds(j * four if isinstance(j, int) else pl.multiple_of(j * four, 16), four)
            tag = lax.broadcasted_iota(jnp.int32, (four, EXT), 1) == me
            pre, up, back = pg[here, :].astype(f32), pu[here, :].astype(f32), bh[there, :]
            sig = jax.nn.sigmoid(pre)
            swish = pre * sig
            hidden = swish * up
            term = jnp.sum(hidden * back, axis=1, keepdims=True)
            pg[here, :] = (back * up * sig * (1.0 + pre * (1.0 - sig))).astype(bf16)
            pu[here, :] = (back * swish).astype(bf16)
            bh[there, :] = hidden
            put(jnp.where(tag, term, 0.0).astype(bf16))

        def put_own(value):
            rb[pl.ds(k * part, four), width:wide] = value

        hidden_rows(0, put_own)

        @pl.loop(1, 4)
        def _(j):
            def put_far(value):
                rs[k, pl.ds(pl.multiple_of((j - 1) * four, 16), four), width:wide] = value

            hidden_rows(j, put_far)

        @pl.loop(0, width // 256)
        def _(n):
            cols = pl.ds(pl.multiple_of(n * 256, 256), 256)
            back = lax.dot_general(
                pg[rows, :], wg[cols, :], OVER_LAST, preferred_element_type=f32
            ) + lax.dot_general(pu[rows, :], wu[cols, :], OVER_LAST, preferred_element_type=f32)
            back = back.astype(bf16)
            rb[pl.ds(k * part, four), cols] = back[:four]
            rs[k, :, cols] = back[four:]

        for j in (1, 2, 3):
            r_copy(k, j).start()
        if k == 3:
            pltpu.make_async_copy(pg.at[rows], last_pre, store_sem.at[4]).start()
            pltpu.make_async_copy(pu.at[rows], last_up, store_sem.at[5]).start()
        ht[:, rows] = bh[...].astype(bf16).T

    def spread(k, i):
        got = jnp.concatenate(
            [rb[pl.ds(k * part + j * four + i * pair, pair), :] for j in range(4)], axis=0
        )
        return jnp.dot(pick_from[k * 2 + i], got, preferred_element_type=f32)

    def returned(k):
        for j in (1, 2, 3):
            r_copy(k, j).wait_recv()

    def back_pair():
        returned(1)
        for i in range(2):
            zs[i] = spread(1, i).astype(bf16)
        pz_copy(1).start()

    def back_near(k):
        returned(k)
        near = spread(k, 1)
        if k == 0:
            pz_copy(1).wait_recv()
            near += zr[1].astype(f32)
        pd[k] = near.astype(bf16)
        pa_copy(k).start()

    def back_far(k):
        pa_copy(k).wait_recv()
        zs[k] = (spread(k, 0) + pa[k].astype(f32)).astype(bf16)
        pz_copy(k).start()

    def forward(u, k):
        z_arrived(u, k)
        if_inner(z_copy(u, k + 1).start)

    def to_neighbour(k):
        a_copy(0, k).start()

    def gather_grads(k):
        a_copy(0, k).wait_recv()
        gather(0, k)

    def gather_tokens(k):
        gather(1, k)

    def tokens_along_z():
        a_copy(1, 0).wait_recv()
        z_first(1)

    def weight_down_grad():
        @pl.loop(0, width // 256)
        def _(n):
            cols = pl.ds(pl.multiple_of(n * 256, 256), 256)
            wd[:, cols] = jnp.dot(ht[...], gr[:, cols], preferred_element_type=f32).astype(bf16)

        pltpu.make_async_copy(wd, out_wd, load_sem.at[2]).start()

    def tile_copy(n, slot):
        cols = pl.ds(pl.multiple_of(n * 256, 256), 256)
        return pltpu.make_async_copy(token_rows.at[pl.ds(0, 3 * part), cols], tile.at[slot], tile_sem.at[slot])

    def weight_in_grads():
        for k in range(3):
            for j in (1, 2, 3):
                c_copy(1, k, j).wait_recv()
        own_rows(2).wait()
        first = pl.ds(0, 3 * part)
        count = width // 256
        tile_copy(0, 0).start()

        @pl.loop(0, count)
        def _(n):
            slot = n % 2

            @pl.when(n + 1 < count)
            def _():
                tile_copy(n + 1, 1 - slot).start()

            tile_copy(n, slot).wait()
            rows = pl.ds(pl.multiple_of(n * 256, 256), 256)
            flipped = tile[slot].T
            wg[rows, :] = jnp.dot(flipped, pg[first, :], preferred_element_type=f32).astype(bf16)
            wu[rows, :] = jnp.dot(flipped, pu[first, :], preferred_element_type=f32).astype(bf16)

        pltpu.make_async_copy(wg, out_wg, load_sem.at[3]).start()
        pltpu.make_async_copy(wu, out_wu, load_sem.at[4]).start()

    def finish():
        pa_copy(0).wait_recv()
        total = spread(0, 0) + pa[0].astype(f32) + zr[0].astype(f32)
        for k in (2, 3):
            pz_arrived(k)
            total += zr[k].astype(f32)
        out_tok[...] = total[:, :width].astype(bf16)
        terms = total[:, width:wide].T
        row8 = lax.broadcasted_iota(jnp.int32, out_gate.shape, 0)
        gates = jnp.zeros(out_gate.shape, f32)
        for r in range(ids_ref.shape[0]):
            term = jnp.where(line == ids_ref[r : r + 1, :], terms, 0.0)
            gates += jnp.where(row8 == r, jnp.sum(term, axis=0, keepdims=True), 0.0)
        out_gate[...] = (gates / gates_ref[...].astype(f32)).astype(bf16)

    gather_grads(0)
    forward(0, 1)
    forward(0, 2)
    to_neighbour(1)
    to_neighbour(2)
    forward(0, 3)
    to_neighbour(3)
    tokens_along_z()
    gather_grads(1)
    gather_grads(2)
    expert(0)
    expert(1)
    gather_grads(3)
    forward(1, 2)
    expert(2)
    forward(1, 1)
    gather_tokens(0)
    back_pair()
    back_near(2)
    expert(3)
    gather_tokens(1)
    gather_tokens(2)
    back_far(2)
    forward(1, 3)
    back_near(3)
    weight_down_grad()
    back_near(0)
    back_far(3)
    gather_tokens(3)
    weight_in_grads()
    finish()

    for u in range(2):
        z_copy(u, 0).wait_send()
        for n in range(1, 5):
            if_inner(z_copy(u, n).wait_send)
        for k in (2, 3):
            for j in (1, 2, 3):
                c_copy(u, k, j).wait_send()
    for j in (1, 2, 3):
        c_copy(1, 3, j).wait_recv()
    own_rows(3).wait()
    a_copy(1, 0).wait_send()
    for k in range(4):
        a_copy(0, k).wait_send()
        if k != 1:
            pa_copy(k).wait_send()
        if k:
            pz_copy(k).wait_send()
        for j in (1, 2, 3):
            r_copy(k, j).wait_send()
    rows = pl.ds(3 * part, part)
    pltpu.make_async_copy(pg.at[rows], last_pre, store_sem.at[4]).wait()
    pltpu.make_async_copy(pu.at[rows], last_up, store_sem.at[5]).wait()
    pltpu.make_async_copy(wd, out_wd, load_sem.at[2]).wait()
    pltpu.make_async_copy(wg, out_wg, load_sem.at[3]).wait()
    pltpu.make_async_copy(wu, out_wu, load_sem.at[4]).wait()


def last_kernel(
    tok_ref, gate_ref, wg_ref, wu_ref, wd_ref, rows_ref, pre_ref, up_ref,
    out_tok, out_gate, out_wg, out_wu, out_wd, wd_held, tok_held, sem,
):
    f32, bf16 = jnp.float32, jnp.bfloat16
    n = pl.program_id(0)
    loads = [
        pltpu.make_async_copy(wd_ref, wd_held, sem.at[0]),
        pltpu.make_async_copy(tok_ref, tok_held, sem.at[1]),
    ]
    stores = [
        pltpu.make_async_copy(wd_held, out_wd, sem.at[2]),
        pltpu.make_async_copy(tok_held, out_tok, sem.at[3]),
    ]

    @pl.when(n == 0)
    def _():
        for copy in loads:
            copy.start()

    @pl.when(n == 1)
    def _():
        for load, store in zip(loads, stores):
            load.wait()
            store.start()

    flipped = rows_ref[...].T
    for ref, into, part in ((pre_ref, out_wg, wg_ref), (up_ref, out_wu, wu_ref)):
        got = jnp.dot(flipped, ref[...], preferred_element_type=f32)
        into[...] = (got + part[...].astype(f32)).astype(bf16)
    out_gate[...] = gate_ref[...]

    @pl.when(n == pl.num_programs(0) - 1)
    def _():
        for copy in stores:
            copy.wait()


def last_part(out_tok, out_gate, out_wg, out_wu, out_wd, rows, pre, up):
    width = out_tok.shape[1]
    part, hid_width = pre.shape
    tall = 512
    steps = width // tall
    start = rows.shape[0] // part - 1

    def down(count, columns):
        return pl.BlockSpec((count, columns), lambda n: (n, 0))

    def whole(a):
        return pl.BlockSpec(a.shape, lambda n: (0, 0))

    parts = [
        pl.BlockSpec(memory_space=pl.ANY), whole(out_gate), down(tall, hid_width),
        down(tall, hid_width), pl.BlockSpec(memory_space=pl.ANY),
    ]
    outs = (out_tok, out_gate, out_wg, out_wu, out_wd)
    return pl.pallas_call(
        last_kernel,
        grid=(steps,),
        out_shape=[jax.ShapeDtypeStruct(a.shape, a.dtype) for a in outs],
        in_specs=parts + [
            pl.BlockSpec((part, tall), lambda n: (start, n)), whole(pre), whole(up)
        ],
        out_specs=parts,
        scratch_shapes=[
            pltpu.VMEM(out_wd.shape, out_wd.dtype), pltpu.VMEM(out_tok.shape, out_tok.dtype),
            pltpu.SemaphoreType.DMA((4,)),
        ],
        compiler_params=pltpu.CompilerParams(vmem_limit_bytes=62 * 1024 * 1024),
    )(*outs, rows, pre, up)


def fused_body(
    tokens, grad_out, expert_ids, pair_slot, gate_weights,
    weight_gate, weight_up, weight_down, saved_gate, saved_up,
):
    f32, bf16 = jnp.float32, jnp.bfloat16
    tok, width = tokens.shape
    wide = width + EXT
    cap, hid_width = saved_gate.shape[1:]
    part = cap // 4
    four = part // 4
    pair = four // 2
    vmem, hbm = pl.BlockSpec(memory_space=pltpu.VMEM), pl.BlockSpec(memory_space=pl.ANY)
    dma = pltpu.SemaphoreType.DMA
    outs = pl.pallas_call(
        fused_kernel,
        out_shape=[
            jax.ShapeDtypeStruct((tok, width), bf16),
            jax.ShapeDtypeStruct(expert_ids.shape[::-1], bf16),
            jax.ShapeDtypeStruct((width, hid_width), bf16),
            jax.ShapeDtypeStruct((width, hid_width), bf16),
            jax.ShapeDtypeStruct((hid_width, width), bf16),
            jax.ShapeDtypeStruct((cap, width), bf16),
            jax.ShapeDtypeStruct((part, hid_width), bf16),
            jax.ShapeDtypeStruct((part, hid_width), bf16),
        ],
        in_specs=[vmem] * 3 + [hbm] * 7,
        out_specs=[vmem] * 2 + [hbm] * 6,
        scratch_shapes=[
            pltpu.VMEM((4, 2, tok, wide), bf16),
            pltpu.VMEM((4, 2, tok, width), bf16),
            pltpu.VMEM((2, 3 * four, width), bf16),
            pltpu.VMEM((2, 4 * four, width), bf16),
            pltpu.VMEM((cap, width), bf16),
            pltpu.VMEM((4, 3 * four, wide), bf16),
            pltpu.VMEM((cap, wide), bf16),
            pltpu.VMEM((4, tok, wide), bf16),
            pltpu.VMEM((4, tok, wide), bf16),
            pltpu.VMEM((4, tok, wide), bf16),
            pltpu.VMEM((4, tok, wide), bf16),
            pltpu.VMEM((width, hid_width), bf16),
            pltpu.VMEM((width, hid_width), bf16),
            pltpu.VMEM((hid_width, width), bf16),
            pltpu.VMEM((cap, hid_width), bf16),
            pltpu.VMEM((cap, hid_width), bf16),
            pltpu.VMEM((part, hid_width), f32),
            pltpu.VMEM((hid_width, cap), bf16),
            pltpu.VMEM((8, 4 * pair, tok), bf16),
            pltpu.VMEM((8, tok, 4 * pair), bf16),
            pltpu.VMEM((4 * pair, EXT), bf16),
            pltpu.VMEM((4 * pair, EXT), bf16),
            pltpu.VMEM((2, 3 * part, 256), bf16),
            dma((5,)), dma((8,)), dma((6,)), dma((2,)),
            dma((13,)), dma((9,)), dma((9,)), dma((9,)),
            dma((24,)), dma((24,)), dma((12,)), dma((12,)),
        ],
        compiler_params=pltpu.CompilerParams(
            collective_id=0, has_side_effects=True, vmem_limit_bytes=62 * 1024 * 1024
        ),
        cost_estimate=pl.CostEstimate(
            flops=10 * cap * width * hid_width, bytes_accessed=20 * cap * width, transcendentals=0
        ),
    )(
        expert_ids.T, pair_slot.T, gate_weights.T, tokens, grad_out,
        weight_gate[0], weight_up[0], weight_down[0], saved_gate[0], saved_up[0],
    )
    out_tok, out_gate, out_wg, out_wu, out_wd = last_part(*outs)
    return (out_tok, out_gate.T, out_wg[None], out_wu[None], out_wd[None])


def body(*args):
    tokens, saved = args[0], args[8]
    if (
        (lax.axis_size("group"), lax.axis_size("member")) == (8, 4)
        and tokens.shape[0] % 128 == 0
        and tokens.shape[1] % 1024 == 0
        and saved.shape[2] % 256 == 0
        and saved.shape[1] % 1536 == 0
    ):
        return fused_body(*args)
    return pair_body(*args)


def solution(mesh):
    flat, deep = P(AXES, None), P(AXES, None, None)
    return jax.shard_map(
        body,
        mesh=mesh,
        in_specs=(flat,) * 5 + (deep,) * 5,
        out_specs=(flat, flat, deep, deep, deep),
        check_vma=False,
    )
```

```python
import jax
import jax.numpy as jnp
from jax import lax
from jax.experimental import pallas as pl
from jax.experimental.pallas import tpu as pltpu
from jax.sharding import PartitionSpec as P

AXES = ("group", "member")


def expert_block(
    token_rows,
    grad_rows,
    route_gate,
    saved_pregate,
    saved_preup,
    weight_gate,
    weight_up,
    weight_down,
):
    pre_gate = saved_pregate.astype(jnp.float32)
    pre_up = saved_preup.astype(jnp.float32)
    gate_sigmoid = jax.nn.sigmoid(pre_gate)
    gate_swish = pre_gate * gate_sigmoid
    hidden = gate_swish * pre_up
    hidden_low = hidden.astype(jnp.bfloat16)
    route_scale = route_gate.astype(jnp.float32)[:, None]
    scaled_grads = (route_scale * grad_rows.astype(jnp.float32)).astype(jnp.bfloat16)
    over_rows = (((0,), (0,)), ((), ()))
    over_features = (((1,), (1,)), ((), ()))
    down_grad = lax.dot_general(
        hidden_low, scaled_grads, over_rows, preferred_element_type=jnp.float32
    )
    back_hidden = lax.dot_general(
        grad_rows, weight_down, over_features, preferred_element_type=jnp.float32
    )
    slot_gate = jnp.sum(hidden * back_hidden, axis=1).astype(jnp.bfloat16)
    hidden_grad = route_scale * back_hidden
    pregate_grad = (
        hidden_grad * pre_up * gate_sigmoid * (1.0 + pre_gate * (1.0 - gate_sigmoid))
    ).astype(jnp.bfloat16)
    preup_grad = (hidden_grad * gate_swish).astype(jnp.bfloat16)
    gate_grad = lax.dot_general(
        token_rows, pregate_grad, over_rows, preferred_element_type=jnp.float32
    )
    up_grad = lax.dot_general(token_rows, preup_grad, over_rows, preferred_element_type=jnp.float32)
    slot_grad = (
        lax.dot_general(
            pregate_grad, weight_gate, over_features, preferred_element_type=jnp.float32
        )
        + lax.dot_general(preup_grad, weight_up, over_features, preferred_element_type=jnp.float32)
    ).astype(jnp.bfloat16)
    return (slot_grad, slot_gate, gate_grad, up_grad, down_grad)


def pair_body(
    tokens,
    grad_out,
    expert_ids,
    pair_slot,
    gate_weights,
    weight_gate,
    weight_up,
    weight_down,
    saved_gate,
    saved_up,
):
    groups = lax.axis_size("group")
    members = lax.axis_size("member")
    experts = groups * members
    tok_rows, model_width = tokens.shape
    route_count = expert_ids.shape[1]
    capacity = saved_gate.shape[1]
    pair_rows = capacity // experts
    token_range = jnp.arange(tok_rows, dtype=jnp.int32)
    dest = (expert_ids * pair_rows + pair_slot).reshape(-1)
    slot_token = (
        jnp.full((experts * pair_rows,), tok_rows, jnp.int32)
        .at[dest]
        .set(jnp.repeat(token_range, route_count))
    )
    send_rows = jnp.take(tokens, slot_token, axis=0, mode="fill", fill_value=0)
    send_grads = jnp.take(grad_out, slot_token, axis=0, mode="fill", fill_value=0)
    send_gates = (
        jnp.zeros((experts * pair_rows,), jnp.bfloat16).at[dest].set(gate_weights.reshape(-1))
    )
    expert_rows, expert_grads, expert_gates = (
        lax.all_to_all(send_rows, ("group", "member"), split_axis=0, concat_axis=0, tiled=True),
        lax.all_to_all(send_grads, ("group", "member"), split_axis=0, concat_axis=0, tiled=True),
        lax.all_to_all(send_gates, ("group", "member"), split_axis=0, concat_axis=0, tiled=True),
    )
    slot_grad, slot_gate, gate_total, up_total, down_total = expert_block(
        expert_rows,
        expert_grads,
        expert_gates,
        saved_gate[0],
        saved_up[0],
        weight_gate[0],
        weight_up[0],
        weight_down[0],
    )
    back_rows, back_terms = (
        lax.all_to_all(slot_grad, ("group", "member"), split_axis=0, concat_axis=0, tiled=True),
        lax.all_to_all(slot_gate, ("group", "member"), split_axis=0, concat_axis=0, tiled=True),
    )
    per_route = jnp.take(back_rows, dest, axis=0).reshape(tok_rows, route_count, model_width)
    grad_tokens = jnp.sum(per_route.astype(jnp.float32), axis=1).astype(jnp.bfloat16)
    grad_gates = jnp.take(back_terms, dest, axis=0).reshape(tok_rows, route_count)
    return (
        grad_tokens,
        grad_gates,
        gate_total[None].astype(jnp.bfloat16),
        up_total[None].astype(jnp.bfloat16),
        down_total[None].astype(jnp.bfloat16),
    )


MESH_ID = pl.DeviceIdType.MESH
EXT = 128
OVER_LAST = (((1,), (1,)), ((), ()))


def fused_kernel(
    ids_ref, slots_ref, gates_ref, tok_hbm, grd_hbm, wg_hbm, wu_hbm, wd_hbm, sa_hbm, sb_hbm,
    out_tok, out_gate, out_wg, out_wu, out_wd, token_rows, last_pre, last_up,
    gd, td, gs, ts, gr, rs, rb, pd, pa, zs, zr, wg, wu, wd, pg, pu, bh, ht, pick_to, pick_from,
    sel, sel_gate, tile, load_sem, row_sem, store_sem, tile_sem,
    z_send, z_recv, a_send, a_recv, c_send, c_recv, r_send, r_recv,
):
    f32, bf16 = jnp.float32, jnp.bfloat16
    tok, width = tok_hbm.shape
    wide = width + EXT
    cap, hid_width = sa_hbm.shape
    part = cap // 4
    four = part // 4
    pair = four // 2
    g, z = lax.axis_index("group"), lax.axis_index("member")
    c, x, y = g % 2, (g // 2) % 2, g // 4
    a, b = x * (1 - c) + y * c, y * (1 - c) + x * c
    me = g * 4 + z
    near_z = z + 1 - 2 * (z % 2)
    inner = (z % 2 + z // 2) % 2

    def place(da, db, dc):
        pa_, pb_ = (1 - a if da else a), (1 - b if db else b)
        pc_ = 1 - c if dc else c
        px, py = pa_ * (1 - c) + pb_ * c, pb_ * (1 - c) + pa_ * c
        return (py * 2 + px) * 2 + pc_

    def plane(k):
        return (z, near_z, 2 - z // 2, 3 - 3 * (z // 2))[k]

    lane_to = ((0, 0, 0), (0, 0, 1), (0, 1, 0), (0, 1, 1))
    lane_from = ((0, 0, 0), (0, 0, 1), (0, 1, 0), (1, 0, 1))

    def source(j, i):
        return ((i, 0, 0), (0, i, 1), (i, 1, 0), (1, i, 1))[j]

    def remote(src, dst, ssem, rsem, group, member):
        return pltpu.make_async_remote_copy(
            src_ref=src, dst_ref=dst, send_sem=ssem, recv_sem=rsem,
            device_id=(group, member), device_id_type=MESH_ID,
        )

    dense = (gd, td)

    hops = ((0, 1, True), (0, 2, False), (1, 3, False), (2, 2, True), (3, 3, True))

    def z_copy(u, n):
        here, there, outward = hops[n]
        src, dst = (gd.at[here, 0], gd.at[there, 0]) if u == 0 else (td.at[here], td.at[there])
        return remote(
            src, dst, z_send.at[u * 5 + n], z_recv.at[u * 3 + there - 1], g,
            near_z if outward else 3 - z,
        )

    def z_arrived(u, k):
        z_copy(u, k - 1).wait_recv()

    def if_inner(act):
        @pl.when(inner == 1)
        def _():
            act()

    def a_copy(u, k):
        n = u * 4 + k
        return remote(
            dense[u].at[k, 0], dense[u].at[k, 1], a_send.at[n], a_recv.at[n], place(1, 0, 0), z
        )

    def c_copy(u, k, j):
        n = (u * 4 + k) * 3 + j - 1
        src, dst = (gs, gr) if u == 0 else (ts, token_rows)
        return remote(
            src.at[k % 2, pl.ds((j - 1) * four, four)], dst.at[pl.ds(k * part + j * four, four)],
            c_send.at[n], c_recv.at[n], place(*lane_to[j]), z,
        )

    def r_copy(k, j):
        n = k * 3 + j - 1
        return remote(
            rs.at[k, pl.ds((j - 1) * four, four)], rb.at[pl.ds(k * part + j * four, four)],
            r_send.at[n], r_recv.at[n], place(*lane_from[j]), z,
        )

    def pa_copy(k):
        return remote(pd.at[k], pa.at[k], a_send.at[5 + k], a_recv.at[5 + k], place(1, 0, 0), z)

    def pz_copy(k):
        if k == 1:
            two = pl.ds(0, 2)
            return remote(zs.at[two], zr.at[two], z_send.at[10], z_recv.at[6], g, near_z)
        there = 3 - inner
        return remote(zs.at[k], zr.at[there], z_send.at[9 + k], z_recv.at[5 + there], g, plane(k))

    def pz_arrived(k):
        remote(zs.at[k], zr.at[k], z_send.at[9 + k], z_recv.at[5 + k], g, plane(k)).wait_recv()

    def own_rows(k):
        return pltpu.make_async_copy(
            ts.at[k % 2, pl.ds(3 * four, four)], token_rows.at[pl.ds(k * part, four)],
            store_sem.at[k],
        )

    load_grd = pltpu.make_async_copy(grd_hbm, gd.at[0, 0, :, pl.ds(0, width)], load_sem.at[0])
    load_tok = pltpu.make_async_copy(tok_hbm, td.at[0, 0], load_sem.at[1])
    load_wd = pltpu.make_async_copy(wd_hbm, wd, load_sem.at[2])
    load_wg = pltpu.make_async_copy(wg_hbm, wg, load_sem.at[3])
    load_wu = pltpu.make_async_copy(wu_hbm, wu, load_sem.at[4])
    load_grd.start()
    load_tok.start()

    barrier = pltpu.get_barrier_semaphore()
    peers = [(place(*p), z) for p in ((1, 0, 0), (1, 0, 1), (0, 1, 0), (0, 1, 1), (0, 0, 1))]
    peers += [(g, plane(k)) for k in (1, 2, 3)]
    for peer in peers:
        pl.semaphore_signal(barrier, inc=1, device_id=peer, device_id_type=MESH_ID)

    line = lax.broadcasted_iota(jnp.int32, (EXT, tok), 0)
    ext = jnp.zeros((EXT, tok), f32)
    for r in range(ids_ref.shape[0]):
        expert_at = ids_ref[r : r + 1, :]
        ext += jnp.where(line == expert_at, gates_ref[r : r + 1, :].astype(f32), 0.0)
        ext += jnp.where(line == expert_at + 32, (slots_ref[r : r + 1, :] + 1).astype(f32), 0.0)
    gd[0, 0, :, width:wide] = ext.T.astype(bf16)
    lane_pair = lax.broadcasted_iota(jnp.int32, (pair, EXT), 1)
    for j in range(4):
        expert_at = place(*lane_to[j]) * 4 + z
        at = pl.ds(j * pair, pair)
        sel[at, :] = jnp.where(lane_pair == expert_at + 32, 1.0, 0.0).astype(bf16)
        sel_gate[at, :] = jnp.where(lane_pair == expert_at, 1.0, 0.0).astype(bf16)

    def z_first(u):
        z_copy(u, 0).start()
        if_inner(z_copy(u, 1).start)

    pl.semaphore_wait(barrier, len(peers))
    load_grd.wait()
    z_first(0)
    a_copy(0, 0).start()
    load_tok.wait()
    a_copy(1, 0).start()
    load_wd.start()
    load_wg.start()
    load_wu.start()
    for k in range(4):
        for j in range(4):
            for i in range(2):
                row = (place(*source(j, i)) * 4 + plane(k)) * pair
                row = pl.ds(pl.multiple_of(row, 16), pair)
                at = pl.ds(k * part + j * four + i * pair, pair)
                pltpu.make_async_copy(sa_hbm.at[row], pg.at[at], row_sem.at[k]).start()
                pltpu.make_async_copy(sb_hbm.at[row], pu.at[at], row_sem.at[4 + k]).start()

    def want(shape, dim):
        at = lax.broadcasted_iota(jnp.int32, shape, dim)
        for _ in range(3):
            at = jnp.where(at >= pair, at - pair, at)
        return (at + 1).astype(f32)

    def gather(u, k):
        if u == 1 and k >= 2:
            own_rows(k - 2).wait()
        if k >= 2:
            for j in (1, 2, 3):
                c_copy(u, k - 2, j).wait_send()
        for i in range(2):
            if u == 0:
                tags = gd[k, i, :, width:wide]
                slot_at = lax.dot_general(sel[...], tags, OVER_LAST, preferred_element_type=f32)
                gate_at = lax.dot_general(sel_gate[...], tags, OVER_LAST, preferred_element_type=f32)
                hit = slot_at == want((4 * pair, tok), 0)
                pick_to[k * 2 + i] = jnp.where(hit, 1.0, 0.0).astype(bf16)
                pick = jnp.where(hit, gate_at, 0.0).astype(bf16)
                slot_at = lax.dot_general(tags, sel[...], OVER_LAST, preferred_element_type=f32)
                pick_from[k * 2 + i] = (slot_at == want((tok, 4 * pair), 1)).astype(bf16)
            if u == 0:
                got = jnp.dot(pick, gd[k, i, :, :width], preferred_element_type=f32)
            else:
                got = jnp.dot(pick_to[k * 2 + i], td[k, i], preferred_element_type=f32)
            got = got.astype(bf16)
            if u == 0:
                gr[pl.ds(k * part + i * pair, pair), :] = got[:pair]
            else:
                ts[k % 2, pl.ds(3 * four + i * pair, pair), :] = got[:pair]
            send = gs if u == 0 else ts
            for j in (1, 2, 3):
                send[k % 2, pl.ds((j - 1) * four + i * pair, pair), :] = got[
                    j * pair : (j + 1) * pair
                ]
        for j in (1, 2, 3):
            c_copy(u, k, j).start()
        if u == 1:
            own_rows(k).start()

    def expert(k):
        rows = pl.ds(k * part, part)
        for j in (1, 2, 3):
            c_copy(0, k, j).wait_recv()
        if k == 0:
            load_wd.wait()
            load_wg.wait()
            load_wu.wait()
        pltpu.make_async_copy(sa_hbm.at[pl.ds(0, part)], pg.at[rows], row_sem.at[k]).wait()
        pltpu.make_async_copy(sb_hbm.at[pl.ds(0, part)], pu.at[rows], row_sem.at[4 + k]).wait()

        @pl.loop(0, hid_width // 256)
        def _(n):
            cols = pl.ds(pl.multiple_of(n * 256, 256), 256)
            bh[:, cols] = lax.dot_general(
                gr[rows, :], wd[cols, :], OVER_LAST, preferred_element_type=f32
            )

        def hidden_rows(j, put):
            at = k * part + j * four
            here = pl.ds(at if isinstance(j, int) else pl.multiple_of(at, 16), four)
            there = pl.ds(j * four if isinstance(j, int) else pl.multiple_of(j * four, 16), four)
            tag = lax.broadcasted_iota(jnp.int32, (four, EXT), 1) == me
            pre, up, back = pg[here, :].astype(f32), pu[here, :].astype(f32), bh[there, :]
            sig = jax.nn.sigmoid(pre)
            swish = pre * sig
            hidden = swish * up
            term = jnp.sum(hidden * back, axis=1, keepdims=True)
            pg[here, :] = (back * up * sig * (1.0 + pre * (1.0 - sig))).astype(bf16)
            pu[here, :] = (back * swish).astype(bf16)
            bh[there, :] = hidden
            put(jnp.where(tag, term, 0.0).astype(bf16))

        def put_own(value):
            rb[pl.ds(k * part, four), width:wide] = value

        hidden_rows(0, put_own)

        @pl.loop(1, 4)
        def _(j):
            def put_far(value):
                rs[k, pl.ds(pl.multiple_of((j - 1) * four, 16), four), width:wide] = value

            hidden_rows(j, put_far)

        @pl.loop(0, width // 256)
        def _(n):
            cols = pl.ds(pl.multiple_of(n * 256, 256), 256)
            back = lax.dot_general(
                pg[rows, :], wg[cols, :], OVER_LAST, preferred_element_type=f32
            ) + lax.dot_general(pu[rows, :], wu[cols, :], OVER_LAST, preferred_element_type=f32)
            back = back.astype(bf16)
            rb[pl.ds(k * part, four), cols] = back[:four]
            rs[k, :, cols] = back[four:]

        for j in (1, 2, 3):
            r_copy(k, j).start()
        if k == 3:
            pltpu.make_async_copy(pg.at[rows], last_pre, store_sem.at[4]).start()
            pltpu.make_async_copy(pu.at[rows], last_up, store_sem.at[5]).start()
        ht[:, rows] = bh[...].astype(bf16).T

    def spread(k, i):
        got = jnp.concatenate(
            [rb[pl.ds(k * part + j * four + i * pair, pair), :] for j in range(4)], axis=0
        )
        return jnp.dot(pick_from[k * 2 + i], got, preferred_element_type=f32)

    def returned(k):
        for j in (1, 2, 3):
            r_copy(k, j).wait_recv()

    def back_pair():
        returned(1)
        for i in range(2):
            zs[i] = spread(1, i).astype(bf16)
        pz_copy(1).start()

    def back_near(k):
        returned(k)
        near = spread(k, 1)
        if k == 0:
            pz_copy(1).wait_recv()
            near += zr[1].astype(f32)
        pd[k] = near.astype(bf16)
        pa_copy(k).start()

    def back_far(k):
        pa_copy(k).wait_recv()
        zs[k] = (spread(k, 0) + pa[k].astype(f32)).astype(bf16)
        pz_copy(k).start()

    def forward(u, k):
        z_arrived(u, k)
        if_inner(z_copy(u, k + 1).start)

    def to_neighbour(k):
        a_copy(0, k).start()

    def gather_grads(k):
        a_copy(0, k).wait_recv()
        gather(0, k)

    def gather_tokens(k):
        gather(1, k)

    def tokens_along_z():
        a_copy(1, 0).wait_recv()
        z_first(1)

    def weight_down_grad():
        @pl.loop(0, width // 256)
        def _(n):
            cols = pl.ds(pl.multiple_of(n * 256, 256), 256)
            wd[:, cols] = jnp.dot(ht[...], gr[:, cols], preferred_element_type=f32).astype(bf16)

        pltpu.make_async_copy(wd, out_wd, load_sem.at[2]).start()

    def tile_copy(n, slot):
        cols = pl.ds(pl.multiple_of(n * 256, 256), 256)
        return pltpu.make_async_copy(token_rows.at[pl.ds(0, 3 * part), cols], tile.at[slot], tile_sem.at[slot])

    def weight_in_grads():
        for k in range(3):
            for j in (1, 2, 3):
                c_copy(1, k, j).wait_recv()
        own_rows(2).wait()
        first = pl.ds(0, 3 * part)
        count = width // 256
        tile_copy(0, 0).start()

        @pl.loop(0, count)
        def _(n):
            slot = n % 2

            @pl.when(n + 1 < count)
            def _():
                tile_copy(n + 1, 1 - slot).start()

            tile_copy(n, slot).wait()
            rows = pl.ds(pl.multiple_of(n * 256, 256), 256)
            flipped = tile[slot].T
            wg[rows, :] = jnp.dot(flipped, pg[first, :], preferred_element_type=f32).astype(bf16)
            wu[rows, :] = jnp.dot(flipped, pu[first, :], preferred_element_type=f32).astype(bf16)

        pltpu.make_async_copy(wg, out_wg, load_sem.at[3]).start()
        pltpu.make_async_copy(wu, out_wu, load_sem.at[4]).start()

    def finish():
        pa_copy(0).wait_recv()
        total = spread(0, 0) + pa[0].astype(f32) + zr[0].astype(f32)
        for k in (2, 3):
            pz_arrived(k)
            total += zr[k].astype(f32)
        out_tok[...] = total[:, :width].astype(bf16)
        terms = total[:, width:wide].T
        row8 = lax.broadcasted_iota(jnp.int32, out_gate.shape, 0)
        gates = jnp.zeros(out_gate.shape, f32)
        for r in range(ids_ref.shape[0]):
            term = jnp.where(line == ids_ref[r : r + 1, :], terms, 0.0)
            gates += jnp.where(row8 == r, jnp.sum(term, axis=0, keepdims=True), 0.0)
        out_gate[...] = (gates / gates_ref[...].astype(f32)).astype(bf16)

    gather_grads(0)
    forward(0, 1)
    to_neighbour(1)
    forward(0, 2)
    tokens_along_z()
    to_neighbour(2)
    gather_grads(1)
    gather_grads(2)
    expert(0)
    forward(0, 3)
    to_neighbour(3)
    expert(1)
    expert(2)
    forward(1, 2)
    gather_grads(3)
    gather_tokens(0)
    forward(1, 1)
    back_pair()
    back_near(2)
    back_far(2)
    expert(3)
    gather_tokens(1)
    gather_tokens(2)
    forward(1, 3)
    back_near(3)
    weight_down_grad()
    back_near(0)
    back_far(3)
    gather_tokens(3)
    weight_in_grads()
    finish()

    for u in range(2):
        z_copy(u, 0).wait_send()
        for n in range(1, 5):
            if_inner(z_copy(u, n).wait_send)
        for k in (2, 3):
            for j in (1, 2, 3):
                c_copy(u, k, j).wait_send()
    for j in (1, 2, 3):
        c_copy(1, 3, j).wait_recv()
    own_rows(3).wait()
    a_copy(1, 0).wait_send()
    for k in range(4):
        a_copy(0, k).wait_send()
        if k != 1:
            pa_copy(k).wait_send()
        if k:
            pz_copy(k).wait_send()
        for j in (1, 2, 3):
            r_copy(k, j).wait_send()
    rows = pl.ds(3 * part, part)
    pltpu.make_async_copy(pg.at[rows], last_pre, store_sem.at[4]).wait()
    pltpu.make_async_copy(pu.at[rows], last_up, store_sem.at[5]).wait()
    pltpu.make_async_copy(wd, out_wd, load_sem.at[2]).wait()
    pltpu.make_async_copy(wg, out_wg, load_sem.at[3]).wait()
    pltpu.make_async_copy(wu, out_wu, load_sem.at[4]).wait()


def last_kernel(
    tok_ref, gate_ref, wg_ref, wu_ref, wd_ref, rows_ref, pre_ref, up_ref,
    out_tok, out_gate, out_wg, out_wu, out_wd, wd_held, tok_held, sem,
):
    f32, bf16 = jnp.float32, jnp.bfloat16
    n = pl.program_id(0)
    loads = [
        pltpu.make_async_copy(wd_ref, wd_held, sem.at[0]),
        pltpu.make_async_copy(tok_ref, tok_held, sem.at[1]),
    ]
    stores = [
        pltpu.make_async_copy(wd_held, out_wd, sem.at[2]),
        pltpu.make_async_copy(tok_held, out_tok, sem.at[3]),
    ]

    @pl.when(n == 0)
    def _():
        for copy in loads:
            copy.start()

    @pl.when(n == 1)
    def _():
        for load, store in zip(loads, stores):
            load.wait()
            store.start()

    flipped = rows_ref[...].T
    for ref, into, part in ((pre_ref, out_wg, wg_ref), (up_ref, out_wu, wu_ref)):
        got = jnp.dot(flipped, ref[...], preferred_element_type=f32)
        into[...] = (got + part[...].astype(f32)).astype(bf16)
    out_gate[...] = gate_ref[...]

    @pl.when(n == pl.num_programs(0) - 1)
    def _():
        for copy in stores:
            copy.wait()


def last_part(out_tok, out_gate, out_wg, out_wu, out_wd, rows, pre, up):
    width = out_tok.shape[1]
    part, hid_width = pre.shape
    tall = 1024
    steps = width // tall
    start = rows.shape[0] // part - 1

    def down(count, columns):
        return pl.BlockSpec((count, columns), lambda n: (n, 0))

    def whole(a):
        return pl.BlockSpec(a.shape, lambda n: (0, 0))

    parts = [
        pl.BlockSpec(memory_space=pl.ANY), whole(out_gate), down(tall, hid_width),
        down(tall, hid_width), pl.BlockSpec(memory_space=pl.ANY),
    ]
    outs = (out_tok, out_gate, out_wg, out_wu, out_wd)
    return pl.pallas_call(
        last_kernel,
        grid=(steps,),
        out_shape=[jax.ShapeDtypeStruct(a.shape, a.dtype) for a in outs],
        in_specs=parts + [
            pl.BlockSpec((part, tall), lambda n: (start, n)), whole(pre), whole(up)
        ],
        out_specs=parts,
        scratch_shapes=[
            pltpu.VMEM(out_wd.shape, out_wd.dtype), pltpu.VMEM(out_tok.shape, out_tok.dtype),
            pltpu.SemaphoreType.DMA((4,)),
        ],
        compiler_params=pltpu.CompilerParams(vmem_limit_bytes=62 * 1024 * 1024),
    )(*outs, rows, pre, up)


def fused_body(
    tokens, grad_out, expert_ids, pair_slot, gate_weights,
    weight_gate, weight_up, weight_down, saved_gate, saved_up,
):
    f32, bf16 = jnp.float32, jnp.bfloat16
    tok, width = tokens.shape
    wide = width + EXT
    cap, hid_width = saved_gate.shape[1:]
    part = cap // 4
    four = part // 4
    pair = four // 2
    vmem, hbm = pl.BlockSpec(memory_space=pltpu.VMEM), pl.BlockSpec(memory_space=pl.ANY)
    dma = pltpu.SemaphoreType.DMA
    outs = pl.pallas_call(
        fused_kernel,
        out_shape=[
            jax.ShapeDtypeStruct((tok, width), bf16),
            jax.ShapeDtypeStruct(expert_ids.shape[::-1], bf16),
            jax.ShapeDtypeStruct((width, hid_width), bf16),
            jax.ShapeDtypeStruct((width, hid_width), bf16),
            jax.ShapeDtypeStruct((hid_width, width), bf16),
            jax.ShapeDtypeStruct((cap, width), bf16),
            jax.ShapeDtypeStruct((part, hid_width), bf16),
            jax.ShapeDtypeStruct((part, hid_width), bf16),
        ],
        in_specs=[vmem] * 3 + [hbm] * 7,
        out_specs=[vmem] * 2 + [hbm] * 6,
        scratch_shapes=[
            pltpu.VMEM((4, 2, tok, wide), bf16),
            pltpu.VMEM((4, 2, tok, width), bf16),
            pltpu.VMEM((2, 3 * four, width), bf16),
            pltpu.VMEM((2, 4 * four, width), bf16),
            pltpu.VMEM((cap, width), bf16),
            pltpu.VMEM((4, 3 * four, wide), bf16),
            pltpu.VMEM((cap, wide), bf16),
            pltpu.VMEM((4, tok, wide), bf16),
            pltpu.VMEM((4, tok, wide), bf16),
            pltpu.VMEM((4, tok, wide), bf16),
            pltpu.VMEM((4, tok, wide), bf16),
            pltpu.VMEM((width, hid_width), bf16),
            pltpu.VMEM((width, hid_width), bf16),
            pltpu.VMEM((hid_width, width), bf16),
            pltpu.VMEM((cap, hid_width), bf16),
            pltpu.VMEM((cap, hid_width), bf16),
            pltpu.VMEM((part, hid_width), f32),
            pltpu.VMEM((hid_width, cap), bf16),
            pltpu.VMEM((8, 4 * pair, tok), bf16),
            pltpu.VMEM((8, tok, 4 * pair), bf16),
            pltpu.VMEM((4 * pair, EXT), bf16),
            pltpu.VMEM((4 * pair, EXT), bf16),
            pltpu.VMEM((2, 3 * part, 256), bf16),
            dma((5,)), dma((8,)), dma((6,)), dma((2,)),
            dma((13,)), dma((9,)), dma((9,)), dma((9,)),
            dma((24,)), dma((24,)), dma((12,)), dma((12,)),
        ],
        compiler_params=pltpu.CompilerParams(
            collective_id=0, has_side_effects=True, vmem_limit_bytes=62 * 1024 * 1024
        ),
        cost_estimate=pl.CostEstimate(
            flops=10 * cap * width * hid_width, bytes_accessed=20 * cap * width, transcendentals=0
        ),
    )(
        expert_ids.T, pair_slot.T, gate_weights.T, tokens, grad_out,
        weight_gate[0], weight_up[0], weight_down[0], saved_gate[0], saved_up[0],
    )
    out_tok, out_gate, out_wg, out_wu, out_wd = last_part(*outs)
    return (out_tok, out_gate.T, out_wg[None], out_wu[None], out_wd[None])


def body(*args):
    tokens, saved = args[0], args[8]
    if (
        (lax.axis_size("group"), lax.axis_size("member")) == (8, 4)
        and tokens.shape[0] % 128 == 0
        and tokens.shape[1] % 2048 == 0
        and saved.shape[2] % 256 == 0
        and saved.shape[1] % 1536 == 0
    ):
        return fused_body(*args)
    return pair_body(*args)


def solution(mesh):
    flat, deep = P(AXES, None), P(AXES, None, None)
    return jax.shard_map(
        body,
        mesh=mesh,
        in_specs=(flat,) * 5 + (deep,) * 5,
        out_specs=(flat, flat, deep, deep, deep),
        check_vma=False,
    )
```
